256 devices in a mesh: dp: 64 (over z, y, core), tensor: 4 (over x).
Axes of the slice: x: 4, y: 4, z: 8, core: 2. Of those that a mesh axis runs over, the one named last changes fastest.
Arguments:
- activations: bfloat16 [16384, 8192], P('dp'), may hold values from -16 to 16
- key_value_grads: bfloat16 [16384, 2, 1024], P('dp', None, 'tensor'), may hold values from -6 to 6
- owner_table: int32 [64], replicated, may hold values from 0 to 63, each once
- left_factors: float32 [4, 64, 512, 512], P('tensor', 'dp'), may hold values from -16 to 16, as said below
- right_factors: float32 [4, 64, 128, 128], P('tensor', 'dp'), may hold values from -16 to 16, as said below
Outputs:
- left_updated: float32 [4, 64, 512, 512], P('tensor', 'dp')
- right_updated: float32 [4, 64, 128, 128], P('tensor', 'dp')
- update: bfloat16 [2, 8192, 1024], P(None, 'dp')
The draws below stay inside these ranges and needn't reach their ends.
Inputs may be any that keep to these rules, and one draw needn't show every extreme that they name: `owner_table`: each block number appears once; slot s lies on index s // 1 of dp. `left_factors`: every block is symmetric positive definite. `right_factors`: every block is symmetric positive definite.
All inputs are finite; a program needn't handle non-finite values.
Results may differ from the reference program's by a relative error of at most 0.012.
The reference program's roundings to bfloat16 on the way (of `direction`) count: a program that leaves them out, or rounds other values in their place, can miss the bound.
Values may be sent and summed in bfloat16 or wider, within the bound.
No kernel may reach another device: no remote copies, remote signals or barrier semaphores. Data moves between devices by JAX's collectives and lax.ppermute only.
A program may use at most 128 MiB of HBM per device.

```python
import jax
import jax.numpy as jnp
from jax import lax

D = 8192
KVW = 1024
BC = 128
BL = 512
ITERS = 8
TOKENS = 16384
TSH = 4
CB = 2
NRB = 16
NBLK = 64


def factor_draw(base_key, salt_value, order_dim, scale_value):
    mixed_key = jax.random.fold_in(base_key, salt_value)
    first_key = jax.random.fold_in(mixed_key, 0)
    base_draw = jax.random.normal(first_key, (TSH, NBLK, order_dim, order_dim), jnp.float32)
    wishart = jnp.einsum('tsik,tsjk->tsij', base_draw, base_draw) / order_dim
    shaped = wishart + 0.25 * jnp.eye(order_dim, dtype=jnp.float32)
    return shaped * scale_value


def draw_left_factors(key, part):
    return factor_draw(key, 11, BL, BC / TOKENS)


def draw_right_factors(key, part):
    return factor_draw(key, 23, BC, BL / TOKENS)


def with_spikes(values, rng, source, target, shards_of, factor):
    def block_of(position):
        return (jnp.arange(values.shape[position]) // (values.shape[position] // shards_of)).reshape((-1,) + (1,) * (values.ndim - 1 - position))

    first = jax.random.permutation(rng, shards_of)[block_of(target)]
    far = (block_of(target) + shards_of // 2) % shards_of
    return jnp.where((block_of(source) == first) | (block_of(source) == far), factor * values, values)


def block_scale(key, dims, shards, low, high):
    def one(position, shards_of):
        steps = jax.random.uniform(jax.random.fold_in(jax.random.fold_in(key, 6), position), (shards_of,), jnp.float32, low / len(shards), high / len(shards))
        return jnp.repeat(jnp.exp(steps), dims[position] // shards_of).reshape((-1,) + (1,) * (len(dims) - position - 1))

    gain = one(*shards[0])
    for cut in shards[1:]:
        gain = gain * one(*cut)
    return gain


def centred(key, extent, width, limit, pieces=(), kind=jnp.bfloat16):
    entries = jax.random.normal(key, extent, jnp.float32) * width
    if len(pieces) > 0:
        entries = block_scale(key, extent, pieces, -0.22, 0.18) * entries
    return jnp.clip(entries, min=-limit, max=limit).astype(kind)


def heavy_noise(rng, dims, scale, reach, cuts, heavy, held_as=jnp.bfloat16):
    values = scale * jax.random.normal(rng, dims, jnp.float32)
    if cuts:
        values = values * block_scale(rng, dims, cuts, -0.22, 0.18)
    return jnp.clip(with_spikes(values, jax.random.fold_in(rng, 3), *heavy), -reach, reach).astype(held_as)


def setup_inputs(seed: int = 0) -> dict:
    arg_keys = jax.random.split(jax.random.key(seed), 6)
    activations = heavy_noise(arg_keys[0], (TOKENS, D), 1.0, 16.0, ((0, 64),), (0, 1, 64, 4.0))
    key_value_grads = centred(arg_keys[1], (TOKENS, 2, KVW), 1.0, 6.0, ((0, 64), (2, 4)))
    owner_table = jax.random.permutation(arg_keys[2], NBLK).astype(jnp.int32)
    left_factors = draw_left_factors(jax.random.fold_in(arg_keys[5], 71), 0)
    right_factors = draw_right_factors(jax.random.fold_in(arg_keys[5], 71), 0)
    return dict(activations=activations, key_value_grads=key_value_grads, owner_table=owner_table, left_factors=left_factors, right_factors=right_factors)


MOMENT_DECAY = 0.9
RIDGE_SHARE = 0.0001
EXACT_MODE = lax.Precision.HIGHEST

def product(left_mat, right_mat):
    return jnp.dot(left_mat, right_mat, precision=EXACT_MODE, preferred_element_type=jnp.float32)

def rounded(matrix):
    narrow = lax.optimization_barrier(matrix.astype(jnp.bfloat16))
    return narrow.astype(jnp.float32)

def coarse_product(left_mat, right_mat):
    return product(rounded(left_mat), rounded(right_mat))

def inverse_root(matrix):
    order_dim = matrix.shape[0]
    identity_mat = jnp.eye(order_dim, dtype=jnp.float32)
    shifted = matrix + RIDGE_SHARE * jnp.trace(matrix) / order_dim * identity_mat
    scaling = 2.5 / jnp.sqrt(jnp.sum(shifted * shifted))
    result = jnp.sqrt(jnp.sqrt(scaling)) * identity_mat
    powered = scaling * shifted
    for iteration in range(ITERS):
        factor = (5.0 * identity_mat - powered) * 0.25
        result = coarse_product(result, factor)
        if iteration + 1 < ITERS:
            squared = coarse_product(factor, factor)
            powered = coarse_product(coarse_product(squared, squared), powered)
    return result

def block_step(inputs):
    gradient, left_old, right_old = inputs
    left_new = MOMENT_DECAY * left_old + (1.0 - MOMENT_DECAY) * product(gradient, gradient.T)
    right_new = MOMENT_DECAY * right_old + (1.0 - MOMENT_DECAY) * product(gradient.T, gradient)
    precond = product(product(inverse_root(left_new), gradient), inverse_root(right_new))
    direction = precond / jnp.sqrt(jnp.mean(precond * precond) + 1e-06)
    return (left_new, right_new, direction.astype(jnp.bfloat16))

def reference(activations, key_value_grads, owner_table, left_factors, right_factors):
    sums = []
    for which in range(2):
        sums.append(jnp.dot(activations.T, key_value_grads[:, which, :], preferred_element_type=jnp.float32) / TOKENS)
    full_grad = jnp.stack(sums)
    canonical = full_grad.reshape(2, NRB, BL, TSH, CB, BC).transpose(3, 0, 1, 4, 2, 5).reshape(TSH, NBLK, BL, BC)
    by_slot = jnp.take(canonical, owner_table, axis=1)
    left_new, right_new, directions = lax.map(block_step, (by_slot.reshape(TSH * NBLK, BL, BC), left_factors.reshape(TSH * NBLK, BL, BL), right_factors.reshape(TSH * NBLK, BC, BC)))
    directions = directions.reshape(TSH, NBLK, BL, BC)
    placed = jnp.zeros((TSH, NBLK, BL, BC), jnp.bfloat16).at[:, owner_table].set(directions)
    update = placed.reshape(TSH, 2, NRB, CB, BL, BC).transpose(1, 2, 4, 0, 3, 5).reshape(2, D, KVW)
    return (left_new.reshape(TSH, NBLK, BL, BL), right_new.reshape(TSH, NBLK, BC, BC), update)
```

```python
import jax
import jax.numpy as jnp
from jax import lax
from jax.experimental import pallas as pl
from jax.experimental.pallas import tpu as pltpu
from jax.sharding import Mesh
from jax.sharding import PartitionSpec as P

ITERS = 8
NZ = 8
NY = 4
DP = ("dp_0", "dp_1", "dp_2")
Z, Y, CORE = DP
F32 = jnp.float32
BF16 = jnp.bfloat16

MOMENT_DECAY = 0.9
RIDGE_SHARE = 0.0001
EXACT_MODE = lax.Precision.HIGHEST


def from_everyone(x, axis):
    size = lax.axis_size(axis)
    return lax.all_to_all(jnp.broadcast_to(x[None], (size, *x.shape)), axis, 0, 0, tiled=True)


def laid_out(parts, dim):
    parts = jnp.moveaxis(parts, 0, dim)
    lengths = parts.shape
    return parts.reshape(*lengths[:dim], lengths[dim] * lengths[dim + 1], *lengths[dim + 2 :])


def collect(x, axis, dim):
    parts = from_everyone(x, axis)
    return laid_out(parts, dim)


def product(left_mat, right_mat):
    return jnp.dot(left_mat, right_mat, precision=EXACT_MODE, preferred_element_type=jnp.float32)


def coarse_product(left_mat, right_mat):
    return jnp.dot(
        left_mat.astype(jnp.bfloat16),
        right_mat.astype(jnp.bfloat16),
        preferred_element_type=jnp.float32,
    )


def inverse_root(matrix):
    order_dim = matrix.shape[0]
    identity_mat = jnp.eye(order_dim, dtype=jnp.float32)
    shifted = matrix + RIDGE_SHARE * jnp.trace(matrix) / order_dim * identity_mat
    scaling = 2.5 / jnp.sqrt(jnp.sum(shifted * shifted))
    result = jnp.sqrt(jnp.sqrt(scaling)) * identity_mat
    powered = scaling * shifted
    for iteration in range(ITERS):
        factor = (5.0 * identity_mat - powered) * 0.25
        result = coarse_product(result, factor)
        if iteration + 1 < ITERS:
            squared = coarse_product(factor, factor)
            powered = coarse_product(coarse_product(squared, squared), powered)
    return result


def block_step(inputs):
    gradient, left_old, right_old = inputs
    left_new = MOMENT_DECAY * left_old + (1.0 - MOMENT_DECAY) * product(gradient, gradient.T)
    right_new = MOMENT_DECAY * right_old + (1.0 - MOMENT_DECAY) * product(gradient.T, gradient)
    precond = product(product(inverse_root(left_new), gradient), inverse_root(right_new))
    direction = precond / jnp.sqrt(jnp.mean(precond * precond) + 1e-06)
    return (left_new, right_new, direction.astype(jnp.bfloat16))


def landing(slot_ids, owner_table, block_order, piece_rows, shard_rows, row_blocks, col_blocks):
    block_ids = jnp.take(owner_table, slot_ids)
    per_projection = row_blocks * col_blocks
    projection = block_ids // per_projection
    remainder = block_ids % per_projection
    row_block = remainder // col_blocks
    column = remainder % col_blocks
    per_block = block_order // piece_rows
    pieces = row_block[:, None] * per_block + jnp.arange(per_block, dtype=jnp.int32)[None, :]
    per_shard = shard_rows // piece_rows
    return (projection, column, pieces // per_shard, pieces % per_shard)


def to_mine(projection, column, target, local_pos, position, per_shard, col_blocks):
    landing_hits = (target == position)[:, :, None, None, None]
    landing_hits = landing_hits & (
        projection[:, None, None, None, None]
        == jnp.arange(2, dtype=jnp.int32)[None, None, :, None, None]
    )
    landing_hits = landing_hits & (
        local_pos[:, :, None, None, None]
        == jnp.arange(per_shard, dtype=jnp.int32)[None, None, None, :, None]
    )
    landing_hits = landing_hits & (
        column[:, None, None, None, None]
        == jnp.arange(col_blocks, dtype=jnp.int32)[None, None, None, None, :]
    )
    return landing_hits.astype(jnp.bfloat16)


def regroup(blocks_data, owner_table, shard_rows, row_blocks, col_blocks, shards):
    slot_count, block_order, width = blocks_data.shape
    cols_block = width // shards
    piece_rows = min(shard_rows, block_order)
    per_block = block_order // piece_rows
    per_shard = shard_rows // piece_rows
    rank_count = lax.axis_size(DP)
    position = lax.axis_index(DP)
    local_ids = position * slot_count + jnp.arange(slot_count, dtype=jnp.int32)
    projection, column, target, local_pos = landing(
        local_ids, owner_table, block_order, piece_rows, shard_rows, row_blocks, col_blocks
    )
    routes = (target[None, :, :] == jnp.arange(rank_count, dtype=jnp.int32)[:, None, None]).astype(
        jnp.bfloat16
    )
    outgoing = jnp.einsum(
        "pim,imqz->piqz",
        routes,
        blocks_data.reshape(slot_count, per_block, piece_rows, width),
        preferred_element_type=jnp.float32,
    ).astype(jnp.bfloat16)
    incoming = lax.all_to_all(outgoing, DP, split_axis=0, concat_axis=0, tiled=True)
    every_id = jnp.arange(rank_count * slot_count, dtype=jnp.int32)
    projection, column, target, local_pos = landing(
        every_id, owner_table, block_order, piece_rows, shard_rows, row_blocks, col_blocks
    )
    landing_hits = jnp.sum(
        to_mine(projection, column, target, local_pos, position, per_shard, col_blocks), axis=1
    )
    assembled = jnp.einsum(
        "sjpc,sqtk->jpqtck",
        landing_hits,
        incoming.reshape(rank_count * slot_count, piece_rows, shards, cols_block),
        preferred_element_type=jnp.float32,
    )
    return assembled.astype(jnp.bfloat16).reshape(2, shard_rows, shards * col_blocks * cols_block)


def shifted(x, axis, step):
    size = lax.axis_size(axis)
    return lax.ppermute(x, axis, [(i, (i + step) % size) for i in range(size)])


def partial_sums(counts, half_cols, acts, acts_peer, kvt, kvt_peer, acts_at, kvt_at):
    rows = kvt.shape[0] // 4
    total = sum(counts)

    def body(acts_at_ref, kvt_at_ref, a_ref, ap_ref, k_ref, kp_ref, *out_refs):
        n = 0
        for count, out_ref in zip(counts, out_refs):
            for i in range(count):
                cols = pl.ds(pl.multiple_of(acts_at_ref[n] * half_cols, half_cols), half_cols)
                lines = pl.ds(pl.multiple_of(kvt_at_ref[n] * rows, rows), rows)
                summed = jnp.dot(k_ref[lines, :], a_ref[:, cols], preferred_element_type=F32)
                summed += jnp.dot(kp_ref[lines, :], ap_ref[:, cols], preferred_element_type=F32)
                out_ref[i] = summed.astype(BF16)
                n += 1

    vmem = pl.BlockSpec(memory_space=pltpu.VMEM)
    smem = pl.BlockSpec(memory_space=pltpu.SMEM)
    return pl.pallas_call(
        body,
        out_shape=[jax.ShapeDtypeStruct((c, rows, half_cols), BF16) for c in counts],
        in_specs=[smem, smem, vmem, vmem, vmem, vmem],
        out_specs=[vmem for _ in counts],
        compiler_params=pltpu.CompilerParams(vmem_limit_bytes=48 * 1024 * 1024),
        name="partial_sums",
    )(acts_at, kvt_at, acts, acts_peer, kvt, kvt_peer)


def wide(*parts):
    total = parts[0].astype(F32)
    for p in parts[1:]:
        total = total + p.astype(F32)
    return total


def added(*parts):
    return wide(*parts).astype(BF16)


def reduce_ring8(v, axis, four_up, four_down, first_up, first_down):
    up = first_up(v[3], shifted(four_up, axis, 1))
    down = first_down(v[-3], shifted(four_down, axis, -1))
    for d in (2, 1):
        up = added(v[d], shifted(up, axis, 1))
        down = added(v[-d], shifted(down, axis, -1))
    return wide(v[0], shifted(up, axis, 1), shifted(down, axis, -1))


def reduce_ring4(v, axis, two_up, two_down, first_up, first_down):
    up = first_up(v[1], shifted(two_up, axis, 1))
    down = first_down(v[-1], shifted(two_down, axis, -1))
    return wide(v[0], shifted(up, axis, 1), shifted(down, axis, -1))


def low_half(base, part):
    h = part.shape[0]
    return jnp.concatenate([added(base[:h], part), base[h:].astype(BF16)], axis=0)


def high_half(base, part):
    h = part.shape[0]
    return jnp.concatenate([base[:h].astype(BF16), added(base[h:], part)], axis=0)


def own_gradient(activations, key_value_grads, owner_table, block_rows, block_cols):
    tokens, features = activations.shape
    half_cols = block_rows // 2
    kvt = key_value_grads.reshape(tokens, -1).T
    pair = [(0, 1), (1, 0)]
    acts_peer = lax.ppermute(activations, CORE, pair)
    kvt_peer = lax.ppermute(kvt, CORE, pair)

    z, y, core = (lax.axis_index(a) for a in DP)
    col_blocks = key_value_grads.shape[2] // block_cols
    row_blocks = features // block_rows

    dz_all = jnp.arange(NZ, dtype=jnp.int32)
    dy_all = jnp.arange(NY, dtype=jnp.int32)
    slots = ((z + dz_all[:, None]) % NZ * NY + (y + dy_all[None, :]) % NY) * 2 + core
    blocks = jnp.take(owner_table, slots)
    projection = blocks // (row_blocks * col_blocks)
    row = blocks % (row_blocks * col_blocks) // col_blocks
    line = projection * col_blocks + blocks % col_blocks

    def listing(pairs):
        dzs = jnp.array([p[0] % NZ for p in pairs], jnp.int32)
        dys = jnp.array([p[1] % NY for p in pairs], jnp.int32)
        halves = jnp.array([p[2] for p in pairs], jnp.int32)
        at = dzs * NY + dys
        return jnp.take(row.reshape(-1), at) * 2 + halves, jnp.take(line.reshape(-1), at)

    def sums(groups):
        a_at, k_at = listing([p for g in groups for p in g])
        counts = [len(g) for g in groups]
        return partial_sums(counts, half_cols, activations, acts_peer, kvt, kvt_peer, a_at, k_at)

    first = [
        [(4, dy, 0) for dy in (0, 1)],
        [(4, dy, 0) for dy in (2, 3)],
        [(dz, 2, 1) for dz in (0, 1, 2, 3)],
        [(dz, 2, 1) for dz in (4, 5, 6, 7)],
    ]
    a_up, a_down, b_up, b_down = sums(first)
    az = (3, -3, 2, -2, 1, -1, 0)
    by = (1, -1, 0)
    rest = [[(dz, dy, 0) for dy in range(NY)] for dz in az]
    rest += [[(dz, dy, 1) for dz in range(NZ)] for dy in by]
    later = sums(rest)
    va = dict(zip(az, later[: len(az)]))
    vb = dict(zip(by, later[len(az) :]))

    ta = reduce_ring8(va, Z, a_up, a_down, low_half, high_half)
    tb = reduce_ring4(vb, Y, b_up, b_down, low_half, high_half)

    h = block_cols // 2
    two = ta[2].astype(BF16)
    ga = reduce_ring4({0: ta[0], 1: ta[1], -1: ta[3]}, Y, two[:h], two[h:], low_half, high_half)
    four = tb[4].astype(BF16)
    vz = {d: tb[d % NZ] for d in range(-3, 4)}
    gb = reduce_ring8(vz, Z, four[:h], four[h:], low_half, high_half)
    return jnp.concatenate([ga, gb], axis=1)


def local(activations, key_value_grads, owner_table, left_factors, right_factors):
    rows_block = left_factors.shape[2]
    cols_block = right_factors.shape[2]
    rank_count = lax.axis_size(DP)
    row_blocks = activations.shape[1] // rows_block
    col_blocks = key_value_grads.shape[2] // cols_block
    shard_rows = activations.shape[1] // rank_count
    inverse_tokens = 1.0 / (activations.shape[0] * rank_count)

    summed = own_gradient(activations, key_value_grads, owner_table, rows_block, cols_block)
    gradient = summed.T * inverse_tokens
    left_new, right_new, directions = block_step((gradient, left_factors[0, 0], right_factors[0, 0]))
    own_rows = regroup(directions[None], owner_table, shard_rows, row_blocks, col_blocks, 1)
    update = collect(own_rows, "tensor", 2)
    return (left_new[None, None], right_new[None, None], update)


def solution(mesh):
    split = Mesh(
        mesh.devices.reshape(8, 4, 2, mesh.shape["tensor"]), ("dp_0", "dp_1", "dp_2", "tensor")
    )
    return jax.shard_map(
        local,
        mesh=split,
        in_specs=(
            P(DP, None),
            P(DP, None, "tensor"),
            P(),
            P("tensor", DP, None, None),
            P("tensor", DP, None, None),
        ),
        out_specs=(P("tensor", DP, None, None), P("tensor", DP, None, None), P(None, DP, None)),
        check_vma=False,
    )
```

```python
import jax
import jax.numpy as jnp
from jax import lax
from jax.experimental import pallas as pl
from jax.experimental.pallas import tpu as pltpu
from jax.sharding import Mesh
from jax.sharding import PartitionSpec as P

ITERS = 8
NZ = 8
NY = 4
DP = ("dp_0", "dp_1", "dp_2")
Z, Y, CORE = DP
F32 = jnp.float32
BF16 = jnp.bfloat16

MOMENT_DECAY = 0.9
RIDGE_SHARE = 0.0001
def shifted(x, axis, step):
    size = lax.axis_size(axis)
    return lax.ppermute(x, axis, [(i, (i + step) % size) for i in range(size)])


def partial_sums(counts, half_cols, acts, acts_peer, kvt, kvt_peer, acts_at, kvt_at):
    rows = kvt.shape[0] // 4
    total = sum(counts)

    def body(acts_at_ref, kvt_at_ref, a_ref, ap_ref, k_ref, kp_ref, *out_refs):
        n = 0
        for count, out_ref in zip(counts, out_refs):
            for i in range(count):
                cols = pl.ds(pl.multiple_of(acts_at_ref[n] * half_cols, half_cols), half_cols)
                lines = pl.ds(pl.multiple_of(kvt_at_ref[n] * rows, rows), rows)
                summed = jnp.dot(k_ref[lines, :], a_ref[:, cols], preferred_element_type=F32)
                summed += jnp.dot(kp_ref[lines, :], ap_ref[:, cols], preferred_element_type=F32)
                out_ref[i] = summed.astype(BF16)
                n += 1

    vmem = pl.BlockSpec(memory_space=pltpu.VMEM)
    smem = pl.BlockSpec(memory_space=pltpu.SMEM)
    return pl.pallas_call(
        body,
        out_shape=[jax.ShapeDtypeStruct((c, rows, half_cols), BF16) for c in counts],
        in_specs=[smem, smem, vmem, vmem, vmem, vmem],
        out_specs=[vmem for _ in counts],
        compiler_params=pltpu.CompilerParams(vmem_limit_bytes=48 * 1024 * 1024),
        name="partial_sums",
    )(acts_at, kvt_at, acts, acts_peer, kvt, kvt_peer)


def wide(*parts):
    total = parts[0].astype(F32)
    for p in parts[1:]:
        total = total + p.astype(F32)
    return total


def added(*parts):
    return wide(*parts).astype(BF16)


def reduce_ring8(v, axis, four_up, four_down, first_up, first_down):
    up = first_up(v[3], shifted(four_up, axis, 1))
    down = first_down(v[-3], shifted(four_down, axis, -1))
    for d in (2, 1):
        up = added(v[d], shifted(up, axis, 1))
        down = added(v[-d], shifted(down, axis, -1))
    return v[0], shifted(up, axis, 1), shifted(down, axis, -1)


def reduce_ring4(v, axis, two_up, two_down, first_up, first_down):
    up = first_up(v[1], shifted(two_up, axis, 1))
    down = first_down(v[-1], shifted(two_down, axis, -1))
    return v[0], shifted(up, axis, 1), shifted(down, axis, -1)


def low_half(base, part):
    h = part.shape[0]
    return jnp.concatenate([added(base[:h], part), base[h:].astype(BF16)], axis=0)


def high_half(base, part):
    h = part.shape[0]
    return jnp.concatenate([base[:h].astype(BF16), added(base[h:], part)], axis=0)


def transposed_sum(refs):
    total = refs[0][...].astype(F32)
    for ref in refs[1:]:
        total = total + ref[...].astype(F32)
    return total


def spread_eye(n):
    return lax.broadcasted_iota(jnp.int32, (n, n), 0) == lax.broadcasted_iota(jnp.int32, (n, n), 1)


def narrow_factor(powered, eye):
    return ((jnp.where(eye, 5.0, 0.0) - powered) * 0.25).astype(BF16)


def coarse(a, b):
    return jnp.dot(a, b, preferred_element_type=F32)


def exact(a, b):
    return jnp.dot(a, b, precision=lax.Precision.HIGHEST, preferred_element_type=F32)


def start_root(matrix, f_ref, m_ref, x_ref):
    n = matrix.shape[0]
    eye = spread_eye(n)
    trace = jnp.sum(jnp.where(eye, matrix, 0.0), keepdims=True)
    shifted = matrix + jnp.where(eye, RIDGE_SHARE * trace / n, 0.0)
    scaling = 2.5 / jnp.sqrt(jnp.sum(shifted * shifted, keepdims=True))
    powered = scaling * shifted
    factor = narrow_factor(powered, eye)
    first = jnp.sqrt(jnp.sqrt(scaling)).astype(BF16).astype(F32)
    f_ref[...] = factor
    m_ref[...] = powered.astype(BF16)
    x_ref[...] = (first * factor.astype(F32)).astype(BF16)


def advance_power(f_ref, m_ref, eye):
    factor = f_ref[...]
    squared = coarse(factor, factor).astype(BF16)
    fourth = coarse(squared, squared).astype(BF16)
    powered = coarse(fourth, m_ref[...])
    f_ref[...] = narrow_factor(powered, eye)
    m_ref[...] = powered.astype(BF16)


def precondition(parts_a, parts_b, left, right, inverse_tokens):
    n_a, n_b = len(parts_a), len(parts_b)
    order, width = left.shape[0], right.shape[0]

    def body(*refs):
        a_refs, b_refs = refs[:n_a], refs[n_a : n_a + n_b]
        left_ref, right_ref, left_out, right_out, dir_ref = refs[n_a + n_b : n_a + n_b + 5]
        g_ref, spread_ref, fl, ml, xl, fr, mr, xr = refs[n_a + n_b + 5 :]
        gt = jnp.concatenate([transposed_sum(a_refs), transposed_sum(b_refs)], axis=1)
        gt = gt * inverse_tokens
        g = gt.T
        g_ref[...] = g
        share = 1.0 - MOMENT_DECAY
        left_new = MOMENT_DECAY * left_ref[...] + share * exact(g, gt)
        left_out[...] = left_new
        start_root(left_new, fl, ml, xl)
        right_new = MOMENT_DECAY * right_ref[...] + share * exact(gt, g)
        right_out[...] = right_new
        start_root(right_new, fr, mr, xr)

        def step(_, carry):
            advance_power(fl, ml, spread_eye(order))
            advance_power(fr, mr, spread_eye(width))
            xl[...] = coarse(xl[...], fl[...]).astype(BF16)
            xr[...] = coarse(xr[...], fr[...]).astype(BF16)
            return carry

        lax.fori_loop(0, ITERS - 2, step, 0)
        advance_power(fl, ml, spread_eye(order))
        advance_power(fr, mr, spread_eye(width))
        left_root = coarse(xl[...], fl[...])
        right_root = coarse(xr[...], fr[...])
        pre = exact(exact(left_root, g_ref[...]), right_root)
        scale = jnp.sqrt(jnp.mean(pre * pre, keepdims=True) + 1e-06)
        g_ref[...] = pre / scale
        pieces = order // 8
        for q in range(4):
            for i in range(2):
                rows = g_ref[pl.ds((q * 2 + i) * pieces, pieces), :]
                spread_ref[pl.ds(q * 2 + i, pieces, stride=8), :] = rows
        dir_ref[...] = spread_ref[...].astype(BF16)

    vmem = pl.BlockSpec(memory_space=pltpu.VMEM)
    square = lambda n: [pltpu.VMEM((n, n), BF16)] * 3
    return pl.pallas_call(
        body,
        out_shape=[
            jax.ShapeDtypeStruct(left.shape, F32),
            jax.ShapeDtypeStruct(right.shape, F32),
            jax.ShapeDtypeStruct((order, width), BF16),
        ],
        in_specs=[vmem] * (n_a + n_b + 2),
        out_specs=[vmem] * 3,
        scratch_shapes=[pltpu.VMEM((order, width), F32)] * 2 + square(order) + square(width),
        compiler_params=pltpu.CompilerParams(vmem_limit_bytes=48 * 1024 * 1024),
        name="precondition",
    )(*parts_a, *parts_b, left, right)

def placed(got, shards):
    pieces, width = got.shape[0], got.shape[3]

    def body(got_ref, out_ref, wide_ref):
        wide_ref[...] = got_ref[...].astype(F32)
        for t in range(shards):
            for j in range(2):
                for c in range(2):
                    for i in range(2):
                        at = t * 8 + j * 4 + c * 2 + i
                        rows = wide_ref[pl.ds(at, pieces, stride=8 * shards), :]
                        cols = pl.ds((t * 2 + c) * width, width)
                        out_ref[j, pl.ds(i * pieces, pieces), cols] = rows.astype(BF16)

    vmem = pl.BlockSpec(memory_space=pltpu.VMEM)
    total = pieces * shards * 8
    return pl.pallas_call(
        body,
        out_shape=jax.ShapeDtypeStruct((2, 2 * pieces, shards * 2 * width), BF16),
        in_specs=[vmem],
        out_specs=vmem,
        scratch_shapes=[pltpu.VMEM((total, width), F32)],
        compiler_params=pltpu.CompilerParams(vmem_limit_bytes=16 * 1024 * 1024),
        name="placed",
    )(got.reshape(total, width))


def routed(directions, owner_table, row_blocks, col_blocks):
    slots = owner_table.shape[0]
    width = directions.shape[1]
    shards = lax.axis_size("tensor")
    held = lax.all_to_all(directions.reshape(slots, 8, width), DP, 0, 0, tiled=True)
    shape = (row_blocks, 4, 2, col_blocks, 2)
    r, q, j, c, i = (lax.broadcasted_iota(jnp.int32, shape, k) for k in range(5))
    wanted = ((((j * row_blocks + r) * col_blocks + c) * 4 + q) * 2 + i).reshape(-1)
    present = (owner_table[:, None] * 8 + jnp.arange(8, dtype=jnp.int32)[None, :]).reshape(-1)
    pick = (wanted[:, None] == present[None, :]).astype(BF16)
    chosen = jnp.dot(pick, held.reshape(slots * 8, width), preferred_element_type=F32)
    chosen = chosen.astype(BF16).reshape(slots, 1, 8, width)
    copies = jnp.broadcast_to(chosen, (slots, shards, 8, width)).reshape(slots * shards, 8, width)
    got = lax.all_to_all(copies, (*DP, "tensor"), 0, 0, tiled=True)
    return placed(got.reshape(slots, shards, 8, width), shards)


def own_gradient(activations, key_value_grads, owner_table, block_rows, block_cols):
    tokens, features = activations.shape
    half_cols = block_rows // 2
    kvt = key_value_grads.reshape(tokens, -1).T
    pair = [(0, 1), (1, 0)]
    acts_peer = lax.ppermute(activations, CORE, pair)
    kvt_peer = lax.ppermute(kvt, CORE, pair)

    z, y, core = (lax.axis_index(a) for a in DP)
    col_blocks = key_value_grads.shape[2] // block_cols
    row_blocks = features // block_rows

    dz_all = jnp.arange(NZ, dtype=jnp.int32)
    dy_all = jnp.arange(NY, dtype=jnp.int32)
    slots = ((z + dz_all[:, None]) % NZ * NY + (y + dy_all[None, :]) % NY) * 2 + core
    blocks = jnp.take(owner_table, slots)
    projection = blocks // (row_blocks * col_blocks)
    row = blocks % (row_blocks * col_blocks) // col_blocks
    line = projection * col_blocks + blocks % col_blocks

    def listing(pairs):
        dzs = jnp.array([p[0] % NZ for p in pairs], jnp.int32)
        dys = jnp.array([p[1] % NY for p in pairs], jnp.int32)
        halves = jnp.array([p[2] for p in pairs], jnp.int32)
        at = dzs * NY + dys
        return jnp.take(row.reshape(-1), at) * 2 + halves, jnp.take(line.reshape(-1), at)

    def sums(groups):
        a_at, k_at = listing([p for g in groups for p in g])
        counts = [len(g) for g in groups]
        return partial_sums(counts, half_cols, activations, acts_peer, kvt, kvt_peer, a_at, k_at)

    first = [
        [(4, dy, 0) for dy in (0, 1)],
        [(4, dy, 0) for dy in (2, 3)],
        [(dz, 2, 1) for dz in (0, 1, 2, 3)],
        [(dz, 2, 1) for dz in (4, 5, 6, 7)],
    ]
    a_up, a_down, b_up, b_down = sums(first)
    az = (3, -3, 2, -2, 1, -1, 0)
    by = (1, -1, 0)
    rest = [[(dz, dy, 0) for dy in range(NY)] for dz in az]
    rest += [[(dz, dy, 1) for dz in range(NZ)] for dy in by]
    later = sums(rest)
    va = dict(zip(az, later[: len(az)]))
    vb = dict(zip(by, later[len(az) :]))

    ta = wide(*reduce_ring8(va, Z, a_up, a_down, low_half, high_half))
    tb = wide(*reduce_ring4(vb, Y, b_up, b_down, low_half, high_half))

    h = block_cols // 2
    two = ta[2].astype(BF16)
    ga = reduce_ring4({0: ta[0], 1: ta[1], -1: ta[3]}, Y, two[:h], two[h:], low_half, high_half)
    four = tb[4].astype(BF16)
    vz = {d: tb[d % NZ] for d in range(-3, 4)}
    gb = reduce_ring8(vz, Z, four[:h], four[h:], low_half, high_half)
    return ga, gb


def local(activations, key_value_grads, owner_table, left_factors, right_factors):
    rows_block = left_factors.shape[2]
    cols_block = right_factors.shape[2]
    row_blocks = activations.shape[1] // rows_block
    col_blocks = key_value_grads.shape[2] // cols_block
    inverse_tokens = 1.0 / (activations.shape[0] * lax.axis_size(DP))

    ga, gb = own_gradient(activations, key_value_grads, owner_table, rows_block, cols_block)
    left_new, right_new, directions = precondition(
        ga, gb, left_factors[0, 0], right_factors[0, 0], inverse_tokens
    )
    update = routed(directions, owner_table, row_blocks, col_blocks)
    return (left_new[None, None], right_new[None, None], update)


def solution(mesh):
    split = Mesh(
        mesh.devices.reshape(8, 4, 2, mesh.shape["tensor"]), ("dp_0", "dp_1", "dp_2", "tensor")
    )
    return jax.shard_map(
        local,
        mesh=split,
        in_specs=(
            P(DP, None),
            P(DP, None, "tensor"),
            P(),
            P("tensor", DP, None, None),
            P("tensor", DP, None, None),
        ),
        out_specs=(P("tensor", DP, None, None), P("tensor", DP, None, None), P(None, DP, None)),
        check_vma=False,
    )
```

```python
import jax
import jax.numpy as jnp
from jax import lax
from jax.experimental import pallas as pl
from jax.experimental.pallas import tpu as pltpu
from jax.sharding import Mesh
from jax.sharding import PartitionSpec as P

ITERS = 8
NZ = 8
NY = 4
DP = ("dp_0", "dp_1", "dp_2")
Z, Y, CORE = DP
F32 = jnp.float32
BF16 = jnp.bfloat16

MOMENT_DECAY = 0.9
RIDGE_SHARE = 0.0001
def directed(x, axis):
    size = lax.axis_size(axis)
    pairs = []
    for i in range(size):
        for core, step in enumerate((1, -1)):
            pairs.append((i * 2 + core, (i + step) % size * 2 + core))
    return lax.ppermute(x, (axis, CORE), pairs)


def swapped(x):
    return lax.ppermute(x, CORE, [(0, 1), (1, 0)])


def wide(*parts):
    total = parts[0].astype(F32)
    for p in parts[1:]:
        total = total + p.astype(F32)
    return total


def added(*parts):
    return wide(*parts).astype(BF16)


def added_first(base, part):
    n = part.shape[0]
    return jnp.concatenate([added(base[:n], part), base[n:].astype(BF16)], axis=0)


def group_a(k):
    if k == 4:
        return [(0, ("fix", 4), ("turn", j), d) for j in range(2) for d in range(2)]
    return [(0, ("sign", k), ("turn", j), d) for j in range(4) for d in range(2)]


def group_b(k):
    if k == 2:
        return [(1, ("turn", j), ("fix", 2), d) for j in range(4) for d in range(2)]
    return [(1, ("turn", j), ("sign", 1), d) for j in range(8) for d in range(2)]


KEPT_A = [(0, ("fix", 0), ("sign", 1), d) for d in range(2)]
KEPT_A += [(0, ("fix", 0), ("fix", dy), 0) for dy in (2, 0)]
KEPT_B = [(1, ("sign", k), ("fix", 0), d) for k in (3, 2, 1) for d in range(2)]
KEPT_B += [(1, ("fix", dz), ("fix", 0), 0) for dz in (4, 0)]


def offset(what, size, core):
    kind, k = what
    if kind == "sign":
        return k + core * (size - 2 * k)
    if kind == "turn":
        return k + core * (size // 2)
    return k


def block_sums(groups, acts, kvt, block_rows, row_blocks, owner_table, before=None):
    half_cols = block_rows // 2
    rows = kvt.shape[0] // 4
    held = F32 if before is None else BF16
    col_blocks = 2

    def body(owner_ref, a_ref, k_ref, *refs):
        base_refs = [] if before is None else refs[: len(groups)]
        out_refs = refs[len(base_refs) :]
        z, y, core = (lax.axis_index(a) for a in DP)
        for g, group in enumerate(groups):
            for n, (half, dz, dy, flip) in enumerate(group):
                to_z = (z + offset(dz, NZ, core)) % NZ
                to_y = (y + offset(dy, NY, core)) % NY
                to_core = core if flip == 0 else 1 - core
                block = owner_ref[(to_z * NY + to_y) * 2 + to_core]
                row = block // col_blocks % row_blocks
                line = block // (row_blocks * col_blocks) * col_blocks + block % col_blocks
                cols = pl.ds(pl.multiple_of((row * 2 + half) * half_cols, half_cols), half_cols)
                lines = pl.ds(pl.multiple_of(line * rows, rows), rows)
                summed = jnp.dot(k_ref[lines, :], a_ref[:, cols], preferred_element_type=F32)
                if before is not None:
                    summed = base_refs[g][n] + summed
                out_refs[g][n] = summed.astype(held)

    vmem = pl.BlockSpec(memory_space=pltpu.VMEM)
    smem = pl.BlockSpec(memory_space=pltpu.SMEM)
    inputs = [] if before is None else list(before)
    return pl.pallas_call(
        body,
        out_shape=[jax.ShapeDtypeStruct((len(g), rows, half_cols), held) for g in groups],
        in_specs=[smem, vmem, vmem] + [vmem] * len(inputs),
        out_specs=[vmem for _ in groups],
        compiler_params=pltpu.CompilerParams(vmem_limit_bytes=40 * 1024 * 1024),
        name="block_sums",
    )(owner_table, acts, kvt, *inputs)


def transposed_sum(refs):
    total = refs[0][...].astype(F32)
    for ref in refs[1:]:
        total = total + ref[...].astype(F32)
    return total


def spread_eye(n):
    return lax.broadcasted_iota(jnp.int32, (n, n), 0) == lax.broadcasted_iota(jnp.int32, (n, n), 1)


def narrow_factor(powered, eye):
    return ((jnp.where(eye, 5.0, 0.0) - powered) * 0.25).astype(BF16)


def coarse(a, b):
    return jnp.dot(a, b, preferred_element_type=F32)


def exact(a, b):
    return jnp.dot(a, b, precision=lax.Precision.HIGHEST, preferred_element_type=F32)


def start_root(matrix, f_ref, m_ref, x_ref):
    n = matrix.shape[0]
    eye = spread_eye(n)
    trace = jnp.sum(jnp.where(eye, matrix, 0.0), keepdims=True)
    shifted = matrix + jnp.where(eye, RIDGE_SHARE * trace / n, 0.0)
    scaling = 2.5 / jnp.sqrt(jnp.sum(shifted * shifted, keepdims=True))
    powered = scaling * shifted
    factor = narrow_factor(powered, eye)
    first = jnp.sqrt(jnp.sqrt(scaling)).astype(BF16).astype(F32)
    f_ref[...] = factor
    m_ref[...] = powered.astype(BF16)
    x_ref[...] = (first * factor.astype(F32)).astype(BF16)


def advance_power(f_ref, m_ref, eye):
    factor = f_ref[...]
    squared = coarse(factor, factor).astype(BF16)
    fourth = coarse(squared, squared).astype(BF16)
    powered = coarse(fourth, m_ref[...])
    f_ref[...] = narrow_factor(powered, eye)
    m_ref[...] = powered.astype(BF16)


def precondition(parts_a, parts_b, left, right, inverse_tokens):
    n_a, n_b = len(parts_a), len(parts_b)
    order, width = left.shape[0], right.shape[0]

    def body(*refs):
        a_refs, b_refs = refs[:n_a], refs[n_a : n_a + n_b]
        left_ref, right_ref, left_out, right_out, dir_ref = refs[n_a + n_b : n_a + n_b + 5]
        g_ref, spread_ref, fl, ml, xl, fr, mr, xr = refs[n_a + n_b + 5 :]
        gt = jnp.concatenate([transposed_sum(a_refs), transposed_sum(b_refs)], axis=1)
        gt = gt * inverse_tokens
        g = gt.T
        g_ref[...] = g
        share = 1.0 - MOMENT_DECAY
        left_new = MOMENT_DECAY * left_ref[...] + share * exact(g, gt)
        left_out[...] = left_new
        start_root(left_new, fl, ml, xl)
        right_new = MOMENT_DECAY * right_ref[...] + share * exact(gt, g)
        right_out[...] = right_new
        start_root(right_new, fr, mr, xr)

        def step(_, carry):
            advance_power(fl, ml, spread_eye(order))
            advance_power(fr, mr, spread_eye(width))
            xl[...] = coarse(xl[...], fl[...]).astype(BF16)
            xr[...] = coarse(xr[...], fr[...]).astype(BF16)
            return carry

        lax.fori_loop(0, ITERS - 2, step, 0)
        advance_power(fl, ml, spread_eye(order))
        advance_power(fr, mr, spread_eye(width))
        left_root = coarse(xl[...], fl[...])
        right_root = coarse(xr[...], fr[...])
        pre = exact(exact(left_root, g_ref[...]), right_root)
        scale = jnp.sqrt(jnp.mean(pre * pre, keepdims=True) + 1e-06)
        g_ref[...] = pre / scale
        pieces = order // 8
        for q in range(4):
            for i in range(2):
                rows = g_ref[pl.ds((q * 2 + i) * pieces, pieces), :]
                spread_ref[pl.ds(q * 2 + i, pieces, stride=8), :] = rows
        dir_ref[...] = spread_ref[...].astype(BF16)

    vmem = pl.BlockSpec(memory_space=pltpu.VMEM)
    square = lambda n: [pltpu.VMEM((n, n), BF16)] * 3
    return pl.pallas_call(
        body,
        out_shape=[
            jax.ShapeDtypeStruct(left.shape, F32),
            jax.ShapeDtypeStruct(right.shape, F32),
            jax.ShapeDtypeStruct((order, width), BF16),
        ],
        in_specs=[vmem] * (n_a + n_b + 2),
        out_specs=[vmem] * 3,
        scratch_shapes=[pltpu.VMEM((order, width), F32)] * 2 + square(order) + square(width),
        compiler_params=pltpu.CompilerParams(vmem_limit_bytes=48 * 1024 * 1024),
        name="precondition",
    )(*parts_a, *parts_b, left, right)

def placed(got, shards):
    pieces, width = got.shape[0], got.shape[3]

    def body(got_ref, out_ref, wide_ref):
        wide_ref[...] = got_ref[...].astype(F32)
        for t in range(shards):
            for j in range(2):
                for c in range(2):
                    for i in range(2):
                        at = t * 8 + j * 4 + c * 2 + i
                        rows = wide_ref[pl.ds(at, pieces, stride=8 * shards), :]
                        cols = pl.ds((t * 2 + c) * width, width)
                        out_ref[j, pl.ds(i * pieces, pieces), cols] = rows.astype(BF16)

    vmem = pl.BlockSpec(memory_space=pltpu.VMEM)
    total = pieces * shards * 8
    return pl.pallas_call(
        body,
        out_shape=jax.ShapeDtypeStruct((2, 2 * pieces, shards * 2 * width), BF16),
        in_specs=[vmem],
        out_specs=vmem,
        scratch_shapes=[pltpu.VMEM((total, width), F32)],
        compiler_params=pltpu.CompilerParams(vmem_limit_bytes=16 * 1024 * 1024),
        name="placed",
    )(got.reshape(total, width))


def routed(directions, owner_table, row_blocks, col_blocks):
    slots = owner_table.shape[0]
    width = directions.shape[1]
    shards = lax.axis_size("tensor")
    held = lax.all_to_all(directions.reshape(slots, 8, width), DP, 0, 0, tiled=True)
    shape = (row_blocks, 4, 2, col_blocks, 2)
    r, q, j, c, i = (lax.broadcasted_iota(jnp.int32, shape, k) for k in range(5))
    wanted = ((((j * row_blocks + r) * col_blocks + c) * 4 + q) * 2 + i).reshape(-1)
    present = (owner_table[:, None] * 8 + jnp.arange(8, dtype=jnp.int32)[None, :]).reshape(-1)
    pick = (wanted[:, None] == present[None, :]).astype(BF16)
    chosen = jnp.dot(pick, held.reshape(slots * 8, width), preferred_element_type=F32)
    chosen = chosen.astype(BF16).reshape(slots, 1, 8, width)
    copies = jnp.broadcast_to(chosen, (slots, shards, 8, width)).reshape(slots * shards, 8, width)
    got = lax.all_to_all(copies, (*DP, "tensor"), 0, 0, tiled=True)
    return placed(got.reshape(slots, shards, 8, width), shards)


def own_gradient(activations, key_value_grads, owner_table, block_rows):
    tokens, features = activations.shape
    row_blocks = features // block_rows
    kvt = key_value_grads.reshape(tokens, -1).T
    acts_peer = swapped(activations)
    kvt_peer = swapped(kvt)

    first = [group_a(4), group_b(2)]
    rest = [group_a(3), group_b(1), group_a(2), group_a(1), KEPT_A, KEPT_B]
    sizes = (block_rows, row_blocks, owner_table)
    own = block_sums(first + rest, activations, kvt, *sizes)
    a4, b2 = block_sums(first, acts_peer, kvt_peer, *sizes, before=own[:2])
    a3, b1, a2, a1, a0, b0 = block_sums(rest, acts_peer, kvt_peer, *sizes, before=own[2:])

    run = added_first(a3, directed(a4, Z))
    run = added(a2, directed(run, Z))
    run = added(a1, directed(run, Z))
    run = directed(run, Z)
    run = run.reshape(2, 2, 2, *run.shape[1:])
    lo, hi = run[0], run[1]
    core = lax.axis_index(CORE)
    even_mine = jnp.where(core == 0, lo[0], hi[0])
    even_far = jnp.where(core == 0, hi[0], lo[0])
    odd_mine = lo[1]
    odd_away = hi[1]
    give = jnp.stack([odd_away[1], odd_away[0], even_far[1], even_mine[1]])
    got = swapped(give)
    keep = jnp.stack([odd_mine[0], odd_mine[1], even_far[0], even_mine[0]])
    kept = wide(a0, keep, got)
    near = added_first(kept[:2], directed(kept[2:3].astype(BF16), Y))
    near = directed(near, Y)
    ga = [kept[3], near[0], swapped(near[1])]

    run = added_first(b1, directed(b2, Y))
    run = directed(run, Y)
    run = run.reshape(2, 4, 2, *run.shape[1:])
    lo, hi = run[0], run[1]
    mine = jnp.where(core == 0, lo[0], hi[0])
    far = jnp.where(core == 0, hi[0], lo[0])
    toward = [jnp.where(core == 0, lo[k], lo[4 - k]) for k in (3, 2, 1)]
    away = [jnp.where(core == 0, hi[4 - k], hi[k]) for k in (3, 2, 1)]
    give = jnp.stack([w[d] for w in away for d in (1, 0)] + [far[1], mine[1]])
    keep = jnp.stack([w[d] for w in toward for d in (0, 1)] + [far[0], mine[0]])
    got = swapped(give)
    kept = wide(b0, keep, got)
    near = added_first(kept[0:2], directed(kept[6:7].astype(BF16), Z))
    near = added(kept[2:4], directed(near, Z))
    near = added(kept[4:6], directed(near, Z))
    near = directed(near, Z)
    gb = [kept[7], near[0], swapped(near[1])]
    return ga, gb


def local(activations, key_value_grads, owner_table, left_factors, right_factors):
    rows_block = left_factors.shape[2]
    cols_block = right_factors.shape[2]
    row_blocks = activations.shape[1] // rows_block
    col_blocks = key_value_grads.shape[2] // cols_block
    inverse_tokens = 1.0 / (activations.shape[0] * lax.axis_size(DP))

    ga, gb = own_gradient(activations, key_value_grads, owner_table, rows_block)
    left_new, right_new, directions = precondition(
        ga, gb, left_factors[0, 0], right_factors[0, 0], inverse_tokens
    )
    update = routed(directions, owner_table, row_blocks, col_blocks)
    return (left_new[None, None], right_new[None, None], update)


def solution(mesh):
    split = Mesh(
        mesh.devices.reshape(8, 4, 2, mesh.shape["tensor"]), ("dp_0", "dp_1", "dp_2", "tensor")
    )
    return jax.shard_map(
        local,
        mesh=split,
        in_specs=(
            P(DP, None),
            P(DP, None, "tensor"),
            P(),
            P("tensor", DP, None, None),
            P("tensor", DP, None, None),
        ),
        out_specs=(P("tensor", DP, None, None), P("tensor", DP, None, None), P(None, DP, None)),
        check_vma=False,
    )
```

```python
import jax
import jax.numpy as jnp
from jax import lax
from jax.experimental import pallas as pl
from jax.experimental.pallas import tpu as pltpu
from jax.sharding import Mesh
from jax.sharding import PartitionSpec as P

ITERS = 8
NZ = 8
NY = 4
DP = ("dp_0", "dp_1", "dp_2")
Z, Y, CORE = DP
F32 = jnp.float32
BF16 = jnp.bfloat16
VMEM_LIMIT = 24 * 1024 * 1024

MOMENT_DECAY = 0.9
RIDGE_SHARE = 0.0001
def directed(x, axis):
    size = lax.axis_size(axis)
    pairs = []
    for i in range(size):
        for core, step in enumerate((1, -1)):
            pairs.append((i * 2 + core, (i + step) % size * 2 + core))
    return lax.ppermute(x, (axis, CORE), pairs)


def swapped(x):
    return lax.ppermute(x, CORE, [(0, 1), (1, 0)])


def wide(*parts):
    total = parts[0].astype(F32)
    for p in parts[1:]:
        total = total + p.astype(F32)
    return total


def added(*parts):
    return wide(*parts).astype(BF16)


def added_inside(base, part, start):
    stop = start + part.shape[0]
    ends = [base[:start].astype(BF16), added(base[start:stop], part), base[stop:].astype(BF16)]
    return jnp.concatenate([e for e in ends if e.shape[0]], axis=0)


def after(x, *others):
    return lax.optimization_barrier((x, *others))[0]


def give_and_keep(near_offsets, fixed):
    back = [("sign", -k) for k in near_offsets]
    ahead = [("sign", k) for k in near_offsets]
    still = [("fix", k) for k in fixed]
    give = [(o, 1) for o in back + still] + [(o, 0) for o in back]
    keep = [(o, 0) for o in ahead + still] + [(o, 1) for o in ahead]
    return give, keep


GIVE_Y, KEEP_Y = give_and_keep((1,), (2, 0))
GIVE_Z, KEEP_Z = give_and_keep((3, 2, 1), (4, 0))
OWN_Y = [e for e in GIVE_Y + KEEP_Y if e[1] == 0]
OWN_Z = [e for e in GIVE_Z + KEEP_Z if e[1] == 0]
FIRST_OWN_Y = (GIVE_Y + KEEP_Y).index(OWN_Y[0])
FIRST_OWN_Z = (GIVE_Z + KEEP_Z).index(OWN_Z[0])


def group_a(dz, entries):
    return [(0, dz, dy, flip) for dy, flip in entries]


def group_b(dy, entries):
    return [(1, dz, dy, flip) for dz, flip in entries]


def offset(what, size, core):
    kind, k = what
    if kind == "sign":
        return size + k - 2 * k * core
    return k


def block_sums(groups, acts, kvt, block_rows, row_blocks, owner_table, before=None):
    half_cols = block_rows // 2
    rows = kvt.shape[0] // 4
    held = F32 if before is None else BF16
    col_blocks = 2

    def body(owner_ref, a_ref, k_ref, *refs):
        base_refs = [] if before is None else refs[: len(groups)]
        out_refs = refs[len(base_refs) :]
        z, y, core = (lax.axis_index(a) for a in DP)
        for g, group in enumerate(groups):
            for n, (half, dz, dy, flip) in enumerate(group):
                to_z = (z + offset(dz, NZ, core)) % NZ
                to_y = (y + offset(dy, NY, core)) % NY
                to_core = core if flip == 0 else 1 - core
                block = owner_ref[(to_z * NY + to_y) * 2 + to_core]
                row = block // col_blocks % row_blocks
                line = block // (row_blocks * col_blocks) * col_blocks + block % col_blocks
                cols = pl.ds(pl.multiple_of((row * 2 + half) * half_cols, half_cols), half_cols)
                lines = pl.ds(pl.multiple_of(line * rows, rows), rows)
                summed = jnp.dot(k_ref[lines, :], a_ref[:, cols], preferred_element_type=F32)
                if before is not None:
                    summed = base_refs[g][n] + summed
                out_refs[g][n] = summed.astype(held)

    vmem = pl.BlockSpec(memory_space=pltpu.VMEM)
    smem = pl.BlockSpec(memory_space=pltpu.SMEM)
    inputs = [] if before is None else list(before)
    return pl.pallas_call(
        body,
        out_shape=[jax.ShapeDtypeStruct((len(g), rows, half_cols), held) for g in groups],
        in_specs=[smem, vmem, vmem] + [vmem] * len(inputs),
        out_specs=[vmem for _ in groups],
        compiler_params=pltpu.CompilerParams(vmem_limit_bytes=VMEM_LIMIT),
        name="block_sums",
    )(owner_table, acts, kvt, *inputs)


def transposed_sum(refs):
    total = refs[0][...].astype(F32)
    for ref in refs[1:]:
        total = total + ref[...].astype(F32)
    return total


def spread_eye(n):
    return lax.broadcasted_iota(jnp.int32, (n, n), 0) == lax.broadcasted_iota(jnp.int32, (n, n), 1)


def narrow_factor(powered, eye):
    return ((jnp.where(eye, 5.0, 0.0) - powered) * 0.25).astype(BF16)


def coarse(a, b):
    return jnp.dot(a, b, preferred_element_type=F32)


def exact(a, b):
    return jnp.dot(a, b, precision=lax.Precision.HIGHEST, preferred_element_type=F32)


def start_root(matrix, f_ref, m_ref, x_ref):
    n = matrix.shape[0]
    eye = spread_eye(n)
    trace = jnp.sum(jnp.where(eye, matrix, 0.0), keepdims=True)
    shifted = matrix + jnp.where(eye, RIDGE_SHARE * trace / n, 0.0)
    scaling = 2.5 / jnp.sqrt(jnp.sum(shifted * shifted, keepdims=True))
    powered = scaling * shifted
    factor = narrow_factor(powered, eye)
    first = jnp.sqrt(jnp.sqrt(scaling)).astype(BF16).astype(F32)
    f_ref[...] = factor
    m_ref[...] = powered.astype(BF16)
    x_ref[...] = (first * factor.astype(F32)).astype(BF16)


def advance_power(f_ref, m_ref, eye):
    factor = f_ref[...]
    squared = coarse(factor, factor).astype(BF16)
    fourth = coarse(squared, squared).astype(BF16)
    powered = coarse(fourth, m_ref[...])
    f_ref[...] = narrow_factor(powered, eye)
    m_ref[...] = powered.astype(BF16)


def precondition(parts_a, parts_b, left, right, inverse_tokens):
    n_a, n_b = len(parts_a), len(parts_b)
    order, width = left.shape[0], right.shape[0]

    def body(*refs):
        a_refs, b_refs = refs[:n_a], refs[n_a : n_a + n_b]
        left_ref, right_ref, left_out, right_out, dir_ref = refs[n_a + n_b : n_a + n_b + 5]
        g_ref, spread_ref, fl, ml, xl, fr, mr, xr = refs[n_a + n_b + 5 :]
        gt = jnp.concatenate([transposed_sum(a_refs), transposed_sum(b_refs)], axis=1)
        gt = gt * inverse_tokens
        g = gt.T
        g_ref[...] = g
        share = 1.0 - MOMENT_DECAY
        left_new = MOMENT_DECAY * left_ref[...] + share * exact(g, gt)
        left_out[...] = left_new
        start_root(left_new, fl, ml, xl)
        right_new = MOMENT_DECAY * right_ref[...] + share * exact(gt, g)
        right_out[...] = right_new
        start_root(right_new, fr, mr, xr)

        def step(_, carry):
            advance_power(fl, ml, spread_eye(order))
            advance_power(fr, mr, spread_eye(width))
            xl[...] = coarse(xl[...], fl[...]).astype(BF16)
            xr[...] = coarse(xr[...], fr[...]).astype(BF16)
            return carry

        lax.fori_loop(0, ITERS - 2, step, 0)
        advance_power(fl, ml, spread_eye(order))
        advance_power(fr, mr, spread_eye(width))
        left_root = coarse(xl[...], fl[...])
        right_root = coarse(xr[...], fr[...])
        pre = exact(exact(left_root, g_ref[...]), right_root)
        scale = jnp.sqrt(jnp.mean(pre * pre, keepdims=True) + 1e-06)
        g_ref[...] = pre / scale
        pieces = order // 8
        for q in range(4):
            for i in range(2):
                rows = g_ref[pl.ds((q * 2 + i) * pieces, pieces), :]
                spread_ref[pl.ds(q * 2 + i, pieces, stride=8), :] = rows
        dir_ref[...] = spread_ref[...].astype(BF16)

    vmem = pl.BlockSpec(memory_space=pltpu.VMEM)
    square = lambda n: [pltpu.VMEM((n, n), BF16)] * 3
    return pl.pallas_call(
        body,
        out_shape=[
            jax.ShapeDtypeStruct(left.shape, F32),
            jax.ShapeDtypeStruct(right.shape, F32),
            jax.ShapeDtypeStruct((order, width), BF16),
        ],
        in_specs=[vmem] * (n_a + n_b + 2),
        out_specs=[vmem] * 3,
        scratch_shapes=[pltpu.VMEM((order, width), F32)] * 2 + square(order) + square(width),
        compiler_params=pltpu.CompilerParams(vmem_limit_bytes=VMEM_LIMIT),
        name="precondition",
    )(*parts_a, *parts_b, left, right)

def placed(got, shards):
    pieces, width = got.shape[0], got.shape[3]

    def body(got_ref, out_ref, wide_ref):
        wide_ref[...] = got_ref[...].astype(F32)
        for t in range(shards):
            for j in range(2):
                for c in range(2):
                    for i in range(2):
                        at = t * 8 + j * 4 + c * 2 + i
                        rows = wide_ref[pl.ds(at, pieces, stride=8 * shards), :]
                        cols = pl.ds((t * 2 + c) * width, width)
                        out_ref[j, pl.ds(i * pieces, pieces), cols] = rows.astype(BF16)

    vmem = pl.BlockSpec(memory_space=pltpu.VMEM)
    total = pieces * shards * 8
    return pl.pallas_call(
        body,
        out_shape=jax.ShapeDtypeStruct((2, 2 * pieces, shards * 2 * width), BF16),
        in_specs=[vmem],
        out_specs=vmem,
        scratch_shapes=[pltpu.VMEM((total, width), F32)],
        compiler_params=pltpu.CompilerParams(vmem_limit_bytes=16 * 1024 * 1024),
        name="placed",
    )(got.reshape(total, width))


def routed(directions, owner_table, row_blocks, col_blocks):
    slots = owner_table.shape[0]
    width = directions.shape[1]
    shards = lax.axis_size("tensor")
    held = lax.all_to_all(directions.reshape(slots, 8, width), DP, 0, 0, tiled=True)
    shape = (row_blocks, 4, 2, col_blocks, 2)
    r, q, j, c, i = (lax.broadcasted_iota(jnp.int32, shape, k) for k in range(5))
    wanted = ((((j * row_blocks + r) * col_blocks + c) * 4 + q) * 2 + i).reshape(-1)
    present = (owner_table[:, None] * 8 + jnp.arange(8, dtype=jnp.int32)[None, :]).reshape(-1)
    pick = (wanted[:, None] == present[None, :]).astype(BF16)
    chosen = jnp.dot(pick, held.reshape(slots * 8, width), preferred_element_type=F32)
    chosen = chosen.astype(BF16).reshape(slots, 1, 8, width)
    copies = jnp.broadcast_to(chosen, (slots, shards, 8, width)).reshape(slots * shards, 8, width)
    got = lax.all_to_all(copies, (*DP, "tensor"), 0, 0, tiled=True)
    return placed(got.reshape(slots, shards, 8, width), shards)


def own_gradient(activations, key_value_grads, owner_table, block_rows):
    tokens, features = activations.shape
    row_blocks = features // block_rows
    kvt = key_value_grads.reshape(tokens, -1).T
    acts_peer = swapped(activations)
    kvt_peer = swapped(kvt)

    all_y, all_z = GIVE_Y + KEEP_Y, GIVE_Z + KEEP_Z
    first = [group_a(("fix", 4), OWN_Y), group_b(("fix", 2), OWN_Z)]
    rest = [group_a(("sign", 3), all_y), group_b(("sign", 1), all_z)]
    rest += [group_a(("sign", 2), all_y), group_a(("sign", 1), all_y)]
    rest += [group_a(("fix", 0), KEEP_Y), group_b(("fix", 0), KEEP_Z)]
    sizes = (block_rows, row_blocks, owner_table)
    own = block_sums(first + rest, activations, kvt, *sizes)
    a4, b2 = block_sums(first, acts_peer, kvt_peer, *sizes, before=own[:2])
    a3, b1, a2, a1, a0, b0 = block_sums(rest, acts_peer, kvt_peer, *sizes, before=own[2:])

    a_run = added_inside(a3, directed(a4, Z), FIRST_OWN_Y)
    b_run = added_inside(b1, directed(b2, Y), FIRST_OWN_Z)
    a_run = added(a2, directed(a_run, Z))
    a_run = added(a1, directed(a_run, Z))
    b_run = directed(b_run, Y)
    n = len(GIVE_Z)
    b = wide(b0, b_run[n:], swapped(b_run[:n]))
    b3, b2, b1, b4, b0 = (b[k] for k in range(5))
    a_run = after(directed(a_run, Z), b)

    b_near = after(directed(b4[None].astype(BF16), Z), a_run)
    b_near = jnp.stack([added(b3, b_near[0]), b[5].astype(BF16)])

    n = len(GIVE_Y)
    a = wide(a0, a_run[n:], swapped(a_run[:n]))
    b_near = after(directed(b_near, Z), a)
    b_near = added(jnp.stack([b2, b[6]]), b_near)
    a_near = directed(a[1:2].astype(BF16), Y)
    a_near = jnp.stack([added(a[0], a_near[0]), a[3].astype(BF16)])
    b_near = after(directed(b_near, Z), a_near)
    b_near = added(jnp.stack([b1, b[7]]), b_near)
    a_near = after(directed(a_near, Y), b_near)
    b_near = directed(b_near, Z)
    ga = [a[2], a_near[0], swapped(a_near[1])]
    gb = [b0, b_near[0], swapped(b_near[1])]
    return ga, gb


def local(activations, key_value_grads, owner_table, left_factors, right_factors):
    rows_block = left_factors.shape[2]
    cols_block = right_factors.shape[2]
    row_blocks = activations.shape[1] // rows_block
    col_blocks = key_value_grads.shape[2] // cols_block
    inverse_tokens = 1.0 / (activations.shape[0] * lax.axis_size(DP))

    ga, gb = own_gradient(activations, key_value_grads, owner_table, rows_block)
    left_new, right_new, directions = precondition(
        ga, gb, left_factors[0, 0], right_factors[0, 0], inverse_tokens
    )
    update = routed(directions, owner_table, row_blocks, col_blocks)
    return (left_new[None, None], right_new[None, None], update)


def solution(mesh):
    split = Mesh(
        mesh.devices.reshape(8, 4, 2, mesh.shape["tensor"]), ("dp_0", "dp_1", "dp_2", "tensor")
    )
    return jax.shard_map(
        local,
        mesh=split,
        in_specs=(
            P(DP, None),
            P(DP, None, "tensor"),
            P(),
            P("tensor", DP, None, None),
            P("tensor", DP, None, None),
        ),
        out_specs=(P("tensor", DP, None, None), P("tensor", DP, None, None), P(None, DP, None)),
        check_vma=False,
    )
```

```python
import jax
import jax.numpy as jnp
from jax import lax
from jax.experimental import pallas as pl
from jax.experimental.pallas import tpu as pltpu
from jax.sharding import Mesh
from jax.sharding import PartitionSpec as P

ITERS = 8
NZ = 8
NY = 4
DP = ("dp_0", "dp_1", "dp_2")
Z, Y, CORE = DP
F32 = jnp.float32
BF16 = jnp.bfloat16
VMEM_LIMIT = 24 * 1024 * 1024

MOMENT_DECAY = 0.9
RIDGE_SHARE = 0.0001
def directed(x, axis, hops=1):
    size = lax.axis_size(axis)
    pairs = []
    for i in range(size):
        for core, step in enumerate((hops, -hops)):
            pairs.append((i * 2 + core, (i + step) % size * 2 + core))
    return lax.ppermute(x, (axis, CORE), pairs)


def swapped(x):
    return lax.ppermute(x, CORE, [(0, 1), (1, 0)])


def wide(*parts):
    total = parts[0].astype(F32)
    for p in parts[1:]:
        total = total + p.astype(F32)
    return total


def added(*parts):
    return wide(*parts).astype(BF16)


def added_inside(base, part, start):
    stop = start + part.shape[0]
    ends = [base[:start].astype(BF16), added(base[start:stop], part), base[stop:].astype(BF16)]
    return jnp.concatenate([e for e in ends if e.shape[0]], axis=0)


def after(x, *others):
    return lax.optimization_barrier((x, *others))[0]


def give_and_keep(near_offsets, fixed):
    back = [("sign", -k) for k in near_offsets]
    ahead = [("sign", k) for k in near_offsets]
    still = [("fix", k) for k in fixed]
    give = [(o, 1) for o in back + still] + [(o, 0) for o in back]
    keep = [(o, 0) for o in ahead + still] + [(o, 1) for o in ahead]
    return give, keep


GIVE_Y, KEEP_Y = give_and_keep((1,), (2, 0))
GIVE_Z, KEEP_Z = give_and_keep((3, 2, 1), (4, 0))
OWN_Y = [e for e in GIVE_Y + KEEP_Y if e[1] == 0]
OWN_Z = [e for e in GIVE_Z + KEEP_Z if e[1] == 0]
FIRST_OWN_Y = (GIVE_Y + KEEP_Y).index(OWN_Y[0])
FIRST_OWN_Z = (GIVE_Z + KEEP_Z).index(OWN_Z[0])


def group_a(dz, entries):
    return [(0, dz, dy, flip) for dy, flip in entries]


def group_b(dy, entries):
    return [(1, dz, dy, flip) for dz, flip in entries]


def offset(what, size, core):
    kind, k = what
    if kind == "sign":
        return size + k - 2 * k * core
    return k


def block_sums(groups, acts, kvt, block_rows, row_blocks, owner_table, before=None):
    half_cols = block_rows // 2
    rows = kvt.shape[0] // 4
    held = F32 if before is None else BF16
    col_blocks = 2

    def body(owner_ref, a_ref, k_ref, *refs):
        base_refs = [] if before is None else refs[: len(groups)]
        out_refs = refs[len(base_refs) :]
        z, y, core = (lax.axis_index(a) for a in DP)
        for g, group in enumerate(groups):
            for n, (half, dz, dy, flip) in enumerate(group):
                to_z = (z + offset(dz, NZ, core)) % NZ
                to_y = (y + offset(dy, NY, core)) % NY
                to_core = core if flip == 0 else 1 - core
                block = owner_ref[(to_z * NY + to_y) * 2 + to_core]
                row = block // col_blocks % row_blocks
                line = block // (row_blocks * col_blocks) * col_blocks + block % col_blocks
                cols = pl.ds(pl.multiple_of((row * 2 + half) * half_cols, half_cols), half_cols)
                lines = pl.ds(pl.multiple_of(line * rows, rows), rows)
                summed = jnp.dot(k_ref[lines, :], a_ref[:, cols], preferred_element_type=F32)
                if before is not None:
                    summed = base_refs[g][n] + summed
                out_refs[g][n] = summed.astype(held)

    vmem = pl.BlockSpec(memory_space=pltpu.VMEM)
    smem = pl.BlockSpec(memory_space=pltpu.SMEM)
    inputs = [] if before is None else list(before)
    return pl.pallas_call(
        body,
        out_shape=[jax.ShapeDtypeStruct((len(g), rows, half_cols), held) for g in groups],
        in_specs=[smem, vmem, vmem] + [vmem] * len(inputs),
        out_specs=[vmem for _ in groups],
        compiler_params=pltpu.CompilerParams(vmem_limit_bytes=VMEM_LIMIT),
        name="block_sums",
    )(owner_table, acts, kvt, *inputs)


def transposed_sum(refs):
    total = refs[0][...].astype(F32)
    for ref in refs[1:]:
        total = total + ref[...].astype(F32)
    return total


def spread_eye(n):
    return lax.broadcasted_iota(jnp.int32, (n, n), 0) == lax.broadcasted_iota(jnp.int32, (n, n), 1)


def narrow_factor(powered, eye):
    return ((jnp.where(eye, 5.0, 0.0) - powered) * 0.25).astype(BF16)


def coarse(a, b):
    return jnp.dot(a, b, preferred_element_type=F32)


def exact(a, b):
    return jnp.dot(a, b, precision=lax.Precision.HIGHEST, preferred_element_type=F32)


def start_root(matrix, f_ref, m_ref, x_ref):
    n = matrix.shape[0]
    eye = spread_eye(n)
    trace = jnp.sum(jnp.where(eye, matrix, 0.0), keepdims=True)
    shifted = matrix + jnp.where(eye, RIDGE_SHARE * trace / n, 0.0)
    scaling = 2.5 / jnp.sqrt(jnp.sum(shifted * shifted, keepdims=True))
    powered = scaling * shifted
    factor = narrow_factor(powered, eye)
    first = jnp.sqrt(jnp.sqrt(scaling)).astype(BF16).astype(F32)
    f_ref[...] = factor
    m_ref[...] = powered.astype(BF16)
    x_ref[...] = (first * factor.astype(F32)).astype(BF16)


def advance_power(f_ref, m_ref, eye):
    factor = f_ref[...]
    squared = coarse(factor, factor).astype(BF16)
    fourth = coarse(squared, squared).astype(BF16)
    powered = coarse(fourth, m_ref[...])
    f_ref[...] = narrow_factor(powered, eye)
    m_ref[...] = powered.astype(BF16)


def precondition(parts_a, parts_b, left, right, inverse_tokens):
    n_a, n_b = len(parts_a), len(parts_b)
    order, width = left.shape[0], right.shape[0]

    def body(*refs):
        a_refs, b_refs = refs[:n_a], refs[n_a : n_a + n_b]
        left_ref, right_ref, left_out, right_out, dir_ref = refs[n_a + n_b : n_a + n_b + 5]
        g_ref, spread_ref, fl, ml, xl, fr, mr, xr = refs[n_a + n_b + 5 :]
        gt = jnp.concatenate([transposed_sum(a_refs), transposed_sum(b_refs)], axis=1)
        gt = gt * inverse_tokens
        g = gt.T
        g_ref[...] = g
        share = 1.0 - MOMENT_DECAY
        left_new = MOMENT_DECAY * left_ref[...] + share * exact(g, gt)
        left_out[...] = left_new
        start_root(left_new, fl, ml, xl)
        right_new = MOMENT_DECAY * right_ref[...] + share * exact(gt, g)
        right_out[...] = right_new
        start_root(right_new, fr, mr, xr)

        def step(_, carry):
            advance_power(fl, ml, spread_eye(order))
            advance_power(fr, mr, spread_eye(width))
            xl[...] = coarse(xl[...], fl[...]).astype(BF16)
            xr[...] = coarse(xr[...], fr[...]).astype(BF16)
            return carry

        lax.fori_loop(0, ITERS - 2, step, 0)
        advance_power(fl, ml, spread_eye(order))
        advance_power(fr, mr, spread_eye(width))
        left_root = coarse(xl[...], fl[...])
        right_root = coarse(xr[...], fr[...])
        pre = exact(exact(left_root, g_ref[...]), right_root)
        scale = jnp.sqrt(jnp.mean(pre * pre, keepdims=True) + 1e-06)
        g_ref[...] = pre / scale
        pieces = order // 8
        for q in range(4):
            for i in range(2):
                rows = g_ref[pl.ds((q * 2 + i) * pieces, pieces), :]
                spread_ref[pl.ds(q * 2 + i, pieces, stride=8), :] = rows
        dir_ref[...] = spread_ref[...].astype(BF16)

    vmem = pl.BlockSpec(memory_space=pltpu.VMEM)
    square = lambda n: [pltpu.VMEM((n, n), BF16)] * 3
    return pl.pallas_call(
        body,
        out_shape=[
            jax.ShapeDtypeStruct(left.shape, F32),
            jax.ShapeDtypeStruct(right.shape, F32),
            jax.ShapeDtypeStruct((order, width), BF16),
        ],
        in_specs=[vmem] * (n_a + n_b + 2),
        out_specs=[vmem] * 3,
        scratch_shapes=[pltpu.VMEM((order, width), F32)] * 2 + square(order) + square(width),
        compiler_params=pltpu.CompilerParams(vmem_limit_bytes=VMEM_LIMIT),
        name="precondition",
    )(*parts_a, *parts_b, left, right)

def placed(got, shards):
    pieces, width = got.shape[0], got.shape[3]

    def body(got_ref, out_ref, wide_ref):
        wide_ref[...] = got_ref[...].astype(F32)
        for t in range(shards):
            for j in range(2):
                for c in range(2):
                    for i in range(2):
                        at = t * 8 + j * 4 + c * 2 + i
                        rows = wide_ref[pl.ds(at, pieces, stride=8 * shards), :]
                        cols = pl.ds((t * 2 + c) * width, width)
                        out_ref[j, pl.ds(i * pieces, pieces), cols] = rows.astype(BF16)

    vmem = pl.BlockSpec(memory_space=pltpu.VMEM)
    total = pieces * shards * 8
    return pl.pallas_call(
        body,
        out_shape=jax.ShapeDtypeStruct((2, 2 * pieces, shards * 2 * width), BF16),
        in_specs=[vmem],
        out_specs=vmem,
        scratch_shapes=[pltpu.VMEM((total, width), F32)],
        compiler_params=pltpu.CompilerParams(vmem_limit_bytes=16 * 1024 * 1024),
        name="placed",
    )(got.reshape(total, width))


def routed(directions, owner_table, row_blocks, col_blocks):
    slots = owner_table.shape[0]
    width = directions.shape[1]
    shards = lax.axis_size("tensor")
    held = lax.all_to_all(directions.reshape(slots, 8, width), DP, 0, 0, tiled=True)
    shape = (row_blocks, 4, 2, col_blocks, 2)
    r, q, j, c, i = (lax.broadcasted_iota(jnp.int32, shape, k) for k in range(5))
    wanted = ((((j * row_blocks + r) * col_blocks + c) * 4 + q) * 2 + i).reshape(-1)
    present = (owner_table[:, None] * 8 + jnp.arange(8, dtype=jnp.int32)[None, :]).reshape(-1)
    pick = (wanted[:, None] == present[None, :]).astype(BF16)
    chosen = jnp.dot(pick, held.reshape(slots * 8, width), preferred_element_type=F32)
    chosen = chosen.astype(BF16).reshape(slots, 1, 8, width)
    copies = jnp.broadcast_to(chosen, (slots, shards, 8, width)).reshape(slots * shards, 8, width)
    got = lax.all_to_all(copies, (*DP, "tensor"), 0, 0, tiled=True)
    return placed(got.reshape(slots, shards, 8, width), shards)


def own_gradient(activations, key_value_grads, owner_table, block_rows):
    tokens, features = activations.shape
    row_blocks = features // block_rows
    kvt = key_value_grads.reshape(tokens, -1).T
    acts_peer = swapped(activations)
    kvt_peer = swapped(kvt)

    all_y, all_z = GIVE_Y + KEEP_Y, GIVE_Z + KEEP_Z
    first = [group_a(("fix", 4), OWN_Y), group_b(("fix", 2), OWN_Z)]
    rest = [group_a(("sign", 3), all_y), group_b(("sign", 1), all_z)]
    rest += [group_a(("sign", 2), all_y), group_a(("sign", 1), all_y)]
    rest += [group_a(("fix", 0), KEEP_Y), group_b(("fix", 0), KEEP_Z)]
    sizes = (block_rows, row_blocks, owner_table)
    own = block_sums(first + rest, activations, kvt, *sizes)
    a4, b2 = block_sums(first, acts_peer, kvt_peer, *sizes, before=own[:2])
    a3, b1, a2, a1, a0, b0 = block_sums(rest, acts_peer, kvt_peer, *sizes, before=own[2:])

    a_run = added_inside(a3, directed(a4, Z), FIRST_OWN_Y)
    b_run = added_inside(b1, directed(b2, Y), FIRST_OWN_Z)
    a_run = added(a2, directed(a_run, Z))
    b_run = directed(b_run, Y)
    a_run = added(a1, directed(a_run, Z))
    n = len(GIVE_Z)
    b = wide(b0, b_run[n:], swapped(b_run[:n]))
    b_far = jnp.stack([b[3], b[0], b[5]]).astype(BF16)
    b_far = directed(b_far, Z, 2)
    b_two = jnp.stack([added(b[1], b_far[0]), b[6].astype(BF16)])
    b_one = jnp.stack([added(b[2], b_far[1]), added(b[7], b_far[2])])

    a_run = after(directed(a_run, Z), b)
    n = len(GIVE_Y)
    a = wide(a0, a_run[n:], swapped(a_run[:n]))
    a_two = a[1:2].astype(BF16)
    a_one = jnp.stack([a[0], a[3]]).astype(BF16)
    b_two = after(directed(b_two, Z, 2), a_two, a_one)
    b_one = after(directed(b_one, Z), a_two, a_one)
    a_two = directed(a_two, Y, 2)
    a_one = directed(a_one, Y)
    b_give = added(b_two[1], b_one[1])
    b_got = swapped(b_give)
    a_got = swapped(a_one[1])
    ga = [a[2], a_two[0], a_one[0], a_got]
    gb = [b[4], b_two[0], b_one[0], b_got]
    return ga, gb


def local(activations, key_value_grads, owner_table, left_factors, right_factors):
    rows_block = left_factors.shape[2]
    cols_block = right_factors.shape[2]
    row_blocks = activations.shape[1] // rows_block
    col_blocks = key_value_grads.shape[2] // cols_block
    inverse_tokens = 1.0 / (activations.shape[0] * lax.axis_size(DP))

    ga, gb = own_gradient(activations, key_value_grads, owner_table, rows_block)
    left_new, right_new, directions = precondition(
        ga, gb, left_factors[0, 0], right_factors[0, 0], inverse_tokens
    )
    update = routed(directions, owner_table, row_blocks, col_blocks)
    return (left_new[None, None], right_new[None, None], update)


def solution(mesh):
    split = Mesh(
        mesh.devices.reshape(8, 4, 2, mesh.shape["tensor"]), ("dp_0", "dp_1", "dp_2", "tensor")
    )
    return jax.shard_map(
        local,
        mesh=split,
        in_specs=(
            P(DP, None),
            P(DP, None, "tensor"),
            P(),
            P("tensor", DP, None, None),
            P("tensor", DP, None, None),
        ),
        out_specs=(P("tensor", DP, None, None), P("tensor", DP, None, None), P(None, DP, None)),
        check_vma=False,
    )
```

```python
import jax
import jax.numpy as jnp
from jax import lax
from jax.experimental import pallas as pl
from jax.experimental.pallas import tpu as pltpu
from jax.sharding import Mesh
from jax.sharding import PartitionSpec as P

ITERS = 8
NZ = 8
NY = 4
DP = ("dp_0", "dp_1", "dp_2")
Z, Y, CORE = DP
F32 = jnp.float32
BF16 = jnp.bfloat16
VMEM_LIMIT = 24 * 1024 * 1024

MOMENT_DECAY = 0.9
RIDGE_SHARE = 0.0001
def directed(x, axis, hops=1):
    size = lax.axis_size(axis)
    pairs = []
    for i in range(size):
        for core, step in enumerate((hops, -hops)):
            pairs.append((i * 2 + core, (i + step) % size * 2 + core))
    return lax.ppermute(x, (axis, CORE), pairs)


def swapped(x):
    return lax.ppermute(x, CORE, [(0, 1), (1, 0)])


def wide(*parts):
    total = parts[0].astype(F32)
    for p in parts[1:]:
        total = total + p.astype(F32)
    return total


def added(*parts):
    return wide(*parts).astype(BF16)


def added_inside(base, part, start):
    stop = start + part.shape[0]
    ends = [base[:start].astype(BF16), added(base[start:stop], part), base[stop:].astype(BF16)]
    return jnp.concatenate([e for e in ends if e.shape[0]], axis=0)


def after(x, *others):
    return lax.optimization_barrier((x, *others))[0]


def give_and_keep(near_offsets, fixed):
    back = [("sign", -k) for k in near_offsets]
    ahead = [("sign", k) for k in near_offsets]
    still = [("fix", k) for k in fixed]
    give = [(o, 1) for o in back + still] + [(o, 0) for o in back]
    keep = [(o, 0) for o in ahead + still] + [(o, 1) for o in ahead]
    return give, keep


GIVE_Y, KEEP_Y = give_and_keep((1,), (2, 0))
GIVE_Z, KEEP_Z = give_and_keep((3, 2, 1), (4, 0))
OWN_Y = [e for e in GIVE_Y + KEEP_Y if e[1] == 0]
OWN_Z = [e for e in GIVE_Z + KEEP_Z if e[1] == 0]
FIRST_OWN_Y = (GIVE_Y + KEEP_Y).index(OWN_Y[0])
FIRST_OWN_Z = (GIVE_Z + KEEP_Z).index(OWN_Z[0])


def group_a(dz, entries):
    return [(0, dz, dy, flip) for dy, flip in entries]


def group_b(dy, entries):
    return [(1, dz, dy, flip) for dz, flip in entries]


def offset(what, size, core):
    kind, k = what
    if kind == "sign":
        return size + k - 2 * k * core
    return k


def block_sums(groups, acts, kvt, block_rows, row_blocks, owner_table, before=None):
    half_cols = block_rows // 2
    rows = kvt.shape[0] // 4
    held = F32 if before is None else BF16
    col_blocks = 2

    def body(owner_ref, a_ref, k_ref, *refs):
        base_refs = [] if before is None else refs[: len(groups)]
        out_refs = refs[len(base_refs) :]
        z, y, core = (lax.axis_index(a) for a in DP)
        for g, group in enumerate(groups):
            for n, (half, dz, dy, flip) in enumerate(group):
                to_z = (z + offset(dz, NZ, core)) % NZ
                to_y = (y + offset(dy, NY, core)) % NY
                to_core = core if flip == 0 else 1 - core
                block = owner_ref[(to_z * NY + to_y) * 2 + to_core]
                row = block // col_blocks % row_blocks
                line = block // (row_blocks * col_blocks) * col_blocks + block % col_blocks
                cols = pl.ds(pl.multiple_of((row * 2 + half) * half_cols, half_cols), half_cols)
                lines = pl.ds(pl.multiple_of(line * rows, rows), rows)
                summed = jnp.dot(k_ref[lines, :], a_ref[:, cols], preferred_element_type=F32)
                if before is not None:
                    summed = base_refs[g][n] + summed
                out_refs[g][n] = summed.astype(held)

    vmem = pl.BlockSpec(memory_space=pltpu.VMEM)
    smem = pl.BlockSpec(memory_space=pltpu.SMEM)
    inputs = [] if before is None else list(before)
    return pl.pallas_call(
        body,
        out_shape=[jax.ShapeDtypeStruct((len(g), rows, half_cols), held) for g in groups],
        in_specs=[smem, vmem, vmem] + [vmem] * len(inputs),
        out_specs=[vmem for _ in groups],
        compiler_params=pltpu.CompilerParams(vmem_limit_bytes=VMEM_LIMIT),
        name="block_sums",
    )(owner_table, acts, kvt, *inputs)


def transposed_sum(refs):
    total = refs[0][...].astype(F32)
    for ref in refs[1:]:
        total = total + ref[...].astype(F32)
    return total


def spread_eye(n):
    return lax.broadcasted_iota(jnp.int32, (n, n), 0) == lax.broadcasted_iota(jnp.int32, (n, n), 1)


def narrow_factor(powered, eye):
    return ((jnp.where(eye, 5.0, 0.0) - powered) * 0.25).astype(BF16)


def coarse(a, b):
    return jnp.dot(a, b, preferred_element_type=F32)


def exact(a, b):
    ah = a.astype(BF16)
    al = (a - ah.astype(F32)).astype(BF16)
    bh = b.astype(BF16)
    bl = (b - bh.astype(F32)).astype(BF16)
    return coarse(ah, bh) + (coarse(ah, bl) + coarse(al, bh))


def start_root(matrix, f_ref, m_ref, x_ref):
    n = matrix.shape[0]
    eye = spread_eye(n)
    trace = jnp.sum(jnp.where(eye, matrix, 0.0), keepdims=True)
    shifted = matrix + jnp.where(eye, RIDGE_SHARE * trace / n, 0.0)
    scaling = 2.5 / jnp.sqrt(jnp.sum(shifted * shifted, keepdims=True))
    powered = scaling * shifted
    factor = narrow_factor(powered, eye)
    first = jnp.sqrt(jnp.sqrt(scaling)).astype(BF16).astype(F32)
    f_ref[...] = factor
    m_ref[...] = powered.astype(BF16)
    x_ref[...] = jnp.where(eye, first, 0.0).astype(BF16)


def precondition(parts_a, parts_b, left, right, inverse_tokens):
    n_a, n_b = len(parts_a), len(parts_b)
    order, width = left.shape[0], right.shape[0]

    def body(*refs):
        a_refs, b_refs = refs[:n_a], refs[n_a : n_a + n_b]
        left_ref, right_ref, left_out, right_out, dir_ref = refs[n_a + n_b : n_a + n_b + 5]
        g_ref, spread_ref, fl, ml, xl, fr, mr, xr = refs[n_a + n_b + 5 :]
        gt = jnp.concatenate([transposed_sum(a_refs), transposed_sum(b_refs)], axis=1)
        gt = gt * inverse_tokens
        g = gt.T
        g_ref[...] = g
        share = 1.0 - MOMENT_DECAY
        left_new = MOMENT_DECAY * left_ref[...] + share * exact(g, gt)
        left_out[...] = left_new
        start_root(left_new, fl, ml, xl)
        right_new = MOMENT_DECAY * right_ref[...] + share * exact(gt, g)
        right_out[...] = right_new
        start_root(right_new, fr, mr, xr)

        eye_l, eye_r = spread_eye(order), spread_eye(width)
        for _ in range(ITERS - 1):
            factor_l, factor_r = fl[...], fr[...]
            squared_l = coarse(factor_l, factor_l).astype(BF16)
            squared_r = coarse(factor_r, factor_r).astype(BF16)
            xl[...] = coarse(xl[...], factor_l).astype(BF16)
            fourth_l = coarse(squared_l, squared_l).astype(BF16)
            fourth_r = coarse(squared_r, squared_r).astype(BF16)
            xr[...] = coarse(xr[...], factor_r).astype(BF16)
            powered_l = coarse(fourth_l, ml[...])
            powered_r = coarse(fourth_r, mr[...])
            fl[...] = narrow_factor(powered_l, eye_l)
            fr[...] = narrow_factor(powered_r, eye_r)
            ml[...] = powered_l.astype(BF16)
            mr[...] = powered_r.astype(BF16)
        left_root = coarse(xl[...], fl[...])
        right_root = coarse(xr[...], fr[...])
        pre = exact(exact(left_root, g_ref[...]), right_root)
        scale = jnp.sqrt(jnp.mean(pre * pre, keepdims=True) + 1e-06)
        g_ref[...] = pre / scale
        pieces = order // 8
        for q in range(4):
            for i in range(2):
                rows = g_ref[pl.ds((q * 2 + i) * pieces, pieces), :]
                spread_ref[pl.ds(q * 2 + i, pieces, stride=8), :] = rows
        dir_ref[...] = spread_ref[...].astype(BF16)

    vmem = pl.BlockSpec(memory_space=pltpu.VMEM)
    square = lambda n: [pltpu.VMEM((n, n), BF16)] * 3
    return pl.pallas_call(
        body,
        out_shape=[
            jax.ShapeDtypeStruct(left.shape, F32),
            jax.ShapeDtypeStruct(right.shape, F32),
            jax.ShapeDtypeStruct((order, width), BF16),
        ],
        in_specs=[vmem] * (n_a + n_b + 2),
        out_specs=[vmem] * 3,
        scratch_shapes=[pltpu.VMEM((order, width), F32)] * 2 + square(order) + square(width),
        compiler_params=pltpu.CompilerParams(vmem_limit_bytes=VMEM_LIMIT),
        name="precondition",
    )(*parts_a, *parts_b, left, right)

def placed(got, shards):
    pieces, width = got.shape[0], got.shape[3]

    def body(got_ref, out_ref, wide_ref):
        wide_ref[...] = got_ref[...].astype(F32)
        for t in range(shards):
            for j in range(2):
                for c in range(2):
                    for i in range(2):
                        at = t * 8 + j * 4 + c * 2 + i
                        rows = wide_ref[pl.ds(at, pieces, stride=8 * shards), :]
                        cols = pl.ds((t * 2 + c) * width, width)
                        out_ref[j, pl.ds(i * pieces, pieces), cols] = rows.astype(BF16)

    vmem = pl.BlockSpec(memory_space=pltpu.VMEM)
    total = pieces * shards * 8
    return pl.pallas_call(
        body,
        out_shape=jax.ShapeDtypeStruct((2, 2 * pieces, shards * 2 * width), BF16),
        in_specs=[vmem],
        out_specs=vmem,
        scratch_shapes=[pltpu.VMEM((total, width), F32)],
        compiler_params=pltpu.CompilerParams(vmem_limit_bytes=16 * 1024 * 1024),
        name="placed",
    )(got.reshape(total, width))


def routed(directions, owner_table, row_blocks, col_blocks):
    slots = owner_table.shape[0]
    width = directions.shape[1]
    shards = lax.axis_size("tensor")
    held = lax.all_to_all(directions.reshape(slots, 8, width), DP, 0, 0, tiled=True)
    shape = (row_blocks, 4, 2, col_blocks, 2)
    r, q, j, c, i = (lax.broadcasted_iota(jnp.int32, shape, k) for k in range(5))
    wanted = ((((j * row_blocks + r) * col_blocks + c) * 4 + q) * 2 + i).reshape(-1)
    present = (owner_table[:, None] * 8 + jnp.arange(8, dtype=jnp.int32)[None, :]).reshape(-1)
    pick = (wanted[:, None] == present[None, :]).astype(BF16)
    chosen = jnp.dot(pick, held.reshape(slots * 8, width), preferred_element_type=F32)
    chosen = chosen.astype(BF16).reshape(slots, 1, 8, width)
    copies = jnp.broadcast_to(chosen, (slots, shards, 8, width)).reshape(slots * shards, 8, width)
    got = lax.all_to_all(copies, (*DP, "tensor"), 0, 0, tiled=True)
    return placed(got.reshape(slots, shards, 8, width), shards)


def own_gradient(activations, key_value_grads, owner_table, block_rows):
    tokens, features = activations.shape
    row_blocks = features // block_rows
    kvt = key_value_grads.reshape(tokens, -1).T
    acts_peer = swapped(activations)
    kvt_peer = swapped(kvt)

    all_y, all_z = GIVE_Y + KEEP_Y, GIVE_Z + KEEP_Z
    first = [group_a(("fix", 4), OWN_Y), group_b(("fix", 2), OWN_Z)]
    rest = [group_a(("sign", 3), all_y), group_b(("sign", 1), all_z)]
    rest += [group_a(("sign", 2), all_y), group_a(("sign", 1), all_y)]
    rest += [group_a(("fix", 0), KEEP_Y), group_b(("fix", 0), KEEP_Z)]
    sizes = (block_rows, row_blocks, owner_table)
    own = block_sums(first + rest, activations, kvt, *sizes)
    a4, b2 = block_sums(first, acts_peer, kvt_peer, *sizes, before=own[:2])
    a3, b1, a2, a1, a0, b0 = block_sums(rest, acts_peer, kvt_peer, *sizes, before=own[2:])

    a_run = added_inside(a3, directed(a4, Z), FIRST_OWN_Y)
    b_run = added_inside(b1, directed(b2, Y), FIRST_OWN_Z)
    a_run = added(a2, directed(a_run, Z))
    b_run = directed(b_run, Y)
    a_run = added(a1, directed(a_run, Z))
    n = len(GIVE_Z)
    b = wide(b0, b_run[n:], swapped(b_run[:n]))
    b_far = jnp.stack([b[3], b[0], b[5]]).astype(BF16)
    b_far = directed(b_far, Z, 2)
    b_two = jnp.stack([added(b[1], b_far[0]), b[6].astype(BF16)])
    b_one = jnp.stack([added(b[2], b_far[1]), added(b[7], b_far[2])])

    a_run = after(directed(a_run, Z), b)
    n = len(GIVE_Y)
    a = wide(a0, a_run[n:], swapped(a_run[:n]))
    a_two = a[1:2].astype(BF16)
    a_one = jnp.stack([a[0], a[3]]).astype(BF16)
    b_two = after(directed(b_two, Z, 2), a_two, a_one)
    b_one = after(directed(b_one, Z), a_two, a_one)
    a_two = directed(a_two, Y, 2)
    a_one = directed(a_one, Y)
    b_give = added(b_two[1], b_one[1])
    b_got = swapped(b_give)
    a_got = swapped(a_one[1])
    ga = [a[2], a_two[0], a_one[0], a_got]
    gb = [b[4], b_two[0], b_one[0], b_got]
    return ga, gb


def local(activations, key_value_grads, owner_table, left_factors, right_factors):
    rows_block = left_factors.shape[2]
    cols_block = right_factors.shape[2]
    row_blocks = activations.shape[1] // rows_block
    col_blocks = key_value_grads.shape[2] // cols_block
    inverse_tokens = 1.0 / (activations.shape[0] * lax.axis_size(DP))

    ga, gb = own_gradient(activations, key_value_grads, owner_table, rows_block)
    left_new, right_new, directions = precondition(
        ga, gb, left_factors[0, 0], right_factors[0, 0], inverse_tokens
    )
    update = routed(directions, owner_table, row_blocks, col_blocks)
    return (left_new[None, None], right_new[None, None], update)


def solution(mesh):
    split = Mesh(
        mesh.devices.reshape(8, 4, 2, mesh.shape["tensor"]), ("dp_0", "dp_1", "dp_2", "tensor")
    )
    return jax.shard_map(
        local,
        mesh=split,
        in_specs=(
            P(DP, None),
            P(DP, None, "tensor"),
            P(),
            P("tensor", DP, None, None),
            P("tensor", DP, None, None),
        ),
        out_specs=(P("tensor", DP, None, None), P("tensor", DP, None, None), P(None, DP, None)),
        check_vma=False,
    )
```

```python
import jax
import jax.numpy as jnp
from jax import lax
from jax.experimental import pallas as pl
from jax.experimental.pallas import tpu as pltpu
from jax.sharding import Mesh
from jax.sharding import PartitionSpec as P

ITERS = 8
NZ = 8
NY = 4
DP = ("dp_0", "dp_1", "dp_2")
Z, Y, CORE = DP
F32 = jnp.float32
BF16 = jnp.bfloat16
VMEM_LIMIT = 24 * 1024 * 1024

MOMENT_DECAY = 0.9
RIDGE_SHARE = 0.0001
def directed(x, axis, hops=1):
    size = lax.axis_size(axis)
    pairs = []
    for i in range(size):
        for core, step in enumerate((hops, -hops)):
            pairs.append((i * 2 + core, (i + step) % size * 2 + core))
    return lax.ppermute(x, (axis, CORE), pairs)


def swapped(x):
    return lax.ppermute(x, CORE, [(0, 1), (1, 0)])


def wide(*parts):
    total = parts[0].astype(F32)
    for p in parts[1:]:
        total = total + p.astype(F32)
    return total


def added(*parts):
    return wide(*parts).astype(BF16)


def added_inside(base, part, start):
    stop = start + part.shape[0]
    ends = [base[:start].astype(BF16), added(base[start:stop], part), base[stop:].astype(BF16)]
    return jnp.concatenate([e for e in ends if e.shape[0]], axis=0)


def after(x, *others):
    return lax.optimization_barrier((x, *others))[0]


def give_and_keep(near_offsets, fixed):
    back = [("sign", -k) for k in near_offsets]
    ahead = [("sign", k) for k in near_offsets]
    still = [("fix", k) for k in fixed]
    give = [(o, 1) for o in back + still] + [(o, 0) for o in back]
    keep = [(o, 0) for o in ahead + still] + [(o, 1) for o in ahead]
    return give, keep


GIVE_Y, KEEP_Y = give_and_keep((1,), (2, 0))
GIVE_Z, KEEP_Z = give_and_keep((3, 2, 1), (4, 0))


def own(entries):
    return [e for e in entries if e[1] == 0]


def own_at(entries):
    return entries.index(own(entries)[0])


def group_a(dz, entries):
    return [(0, dz, dy, flip) for dy, flip in entries]


def group_b(dy, entries):
    return [(1, dz, dy, flip) for dz, flip in entries]


def offset(what, size, core):
    kind, k = what
    if kind == "sign":
        return size + k - 2 * k * core
    return k


def block_sums(groups, acts, kvt, block_rows, row_blocks, owner_table, before=None):
    half_cols = block_rows // 2
    rows = kvt.shape[0] // 4
    held = F32 if before is None else BF16
    col_blocks = 2

    def body(owner_ref, a_ref, k_ref, *refs):
        base_refs = [] if before is None else refs[: len(groups)]
        out_refs = refs[len(base_refs) :]
        z, y, core = (lax.axis_index(a) for a in DP)
        for g, group in enumerate(groups):
            for n, (half, dz, dy, flip) in enumerate(group):
                to_z = (z + offset(dz, NZ, core)) % NZ
                to_y = (y + offset(dy, NY, core)) % NY
                to_core = core if flip == 0 else 1 - core
                block = owner_ref[(to_z * NY + to_y) * 2 + to_core]
                row = block // col_blocks % row_blocks
                line = block // (row_blocks * col_blocks) * col_blocks + block % col_blocks
                cols = pl.ds(pl.multiple_of((row * 2 + half) * half_cols, half_cols), half_cols)
                lines = pl.ds(pl.multiple_of(line * rows, rows), rows)
                summed = jnp.dot(k_ref[lines, :], a_ref[:, cols], preferred_element_type=F32)
                if before is not None:
                    summed = base_refs[g][n] + summed
                out_refs[g][n] = summed.astype(held)

    vmem = pl.BlockSpec(memory_space=pltpu.VMEM)
    smem = pl.BlockSpec(memory_space=pltpu.SMEM)
    inputs = [] if before is None else list(before)
    count = sum(len(g) for g in groups)
    moved = acts.size * 2 + kvt.size * 2 + count * rows * half_cols * (4 if before is None else 6)
    cost = pl.CostEstimate(
        flops=2 * count * rows * half_cols * acts.shape[0], transcendentals=0, bytes_accessed=moved
    )
    return pl.pallas_call(
        body,
        out_shape=[jax.ShapeDtypeStruct((len(g), rows, half_cols), held) for g in groups],
        in_specs=[smem, vmem, vmem] + [vmem] * len(inputs),
        out_specs=[vmem for _ in groups],
        compiler_params=pltpu.CompilerParams(vmem_limit_bytes=VMEM_LIMIT),
        cost_estimate=cost,
        name="block_sums",
    )(owner_table, acts, kvt, *inputs)


def transposed_sum(refs):
    total = refs[0][...].astype(F32)
    for ref in refs[1:]:
        total = total + ref[...].astype(F32)
    return total


def spread_eye(n):
    return lax.broadcasted_iota(jnp.int32, (n, n), 0) == lax.broadcasted_iota(jnp.int32, (n, n), 1)


def narrow_factor(powered, eye):
    return ((jnp.where(eye, 5.0, 0.0) - powered) * 0.25).astype(BF16)


def coarse(a, b):
    return jnp.dot(a, b, preferred_element_type=F32)


def exact(a, b):
    ah = a.astype(BF16)
    al = (a - ah.astype(F32)).astype(BF16)
    bh = b.astype(BF16)
    bl = (b - bh.astype(F32)).astype(BF16)
    return coarse(ah, bh) + (coarse(ah, bl) + coarse(al, bh))


def start_root(matrix, f_ref, m_ref, x_ref):
    n = matrix.shape[0]
    eye = spread_eye(n)
    trace = jnp.sum(jnp.where(eye, matrix, 0.0), keepdims=True)
    shifted = matrix + jnp.where(eye, RIDGE_SHARE * trace / n, 0.0)
    scaling = 2.5 / jnp.sqrt(jnp.sum(shifted * shifted, keepdims=True))
    powered = scaling * shifted
    factor = narrow_factor(powered, eye)
    first = jnp.sqrt(jnp.sqrt(scaling)).astype(BF16).astype(F32)
    f_ref[...] = factor
    m_ref[...] = powered.astype(BF16)
    x_ref[...] = jnp.where(eye, first, 0.0).astype(BF16)


def precondition(parts_a, parts_b, left, right, inverse_tokens):
    n_a, n_b = len(parts_a), len(parts_b)
    order, width = left.shape[0], right.shape[0]

    def body(*refs):
        a_refs, b_refs = refs[:n_a], refs[n_a : n_a + n_b]
        left_ref, right_ref, left_out, right_out, dir_ref = refs[n_a + n_b : n_a + n_b + 5]
        g_ref, spread_ref, fl, ml, xl, fr, mr, xr = refs[n_a + n_b + 5 :]
        gt = jnp.concatenate([transposed_sum(a_refs), transposed_sum(b_refs)], axis=1)
        gt = gt * inverse_tokens
        g = gt.T
        g_ref[...] = g
        share = 1.0 - MOMENT_DECAY
        left_new = MOMENT_DECAY * left_ref[...] + share * exact(g, gt)
        left_out[...] = left_new
        start_root(left_new, fl, ml, xl)
        right_new = MOMENT_DECAY * right_ref[...] + share * exact(gt, g)
        right_out[...] = right_new
        start_root(right_new, fr, mr, xr)

        eye_l, eye_r = spread_eye(order), spread_eye(width)
        for _ in range(ITERS - 1):
            factor_l, factor_r = fl[...], fr[...]
            squared_l = coarse(factor_l, factor_l).astype(BF16)
            squared_r = coarse(factor_r, factor_r).astype(BF16)
            xl[...] = coarse(xl[...], factor_l).astype(BF16)
            fourth_l = coarse(squared_l, squared_l).astype(BF16)
            fourth_r = coarse(squared_r, squared_r).astype(BF16)
            xr[...] = coarse(xr[...], factor_r).astype(BF16)
            powered_l = coarse(fourth_l, ml[...])
            powered_r = coarse(fourth_r, mr[...])
            fl[...] = narrow_factor(powered_l, eye_l)
            fr[...] = narrow_factor(powered_r, eye_r)
            ml[...] = powered_l.astype(BF16)
            mr[...] = powered_r.astype(BF16)
        left_root = coarse(xl[...], fl[...])
        right_root = coarse(xr[...], fr[...])
        pre = exact(exact(left_root, g_ref[...]), right_root)
        scale = jnp.sqrt(jnp.mean(pre * pre, keepdims=True) + 1e-06)
        g_ref[...] = pre / scale
        pieces = order // 8
        for q in range(4):
            for i in range(2):
                rows = g_ref[pl.ds((q * 2 + i) * pieces, pieces), :]
                spread_ref[pl.ds(q * 2 + i, pieces, stride=8), :] = rows
        dir_ref[...] = spread_ref[...].astype(BF16)

    vmem = pl.BlockSpec(memory_space=pltpu.VMEM)
    square = lambda n: [pltpu.VMEM((n, n), BF16)] * 3
    return pl.pallas_call(
        body,
        out_shape=[
            jax.ShapeDtypeStruct(left.shape, F32),
            jax.ShapeDtypeStruct(right.shape, F32),
            jax.ShapeDtypeStruct((order, width), BF16),
        ],
        in_specs=[vmem] * (n_a + n_b + 2),
        out_specs=[vmem] * 3,
        scratch_shapes=[pltpu.VMEM((order, width), F32)] * 2 + square(order) + square(width),
        compiler_params=pltpu.CompilerParams(vmem_limit_bytes=VMEM_LIMIT),
        name="precondition",
    )(*parts_a, *parts_b, left, right)

def placed(got, shards):
    pieces, width = got.shape[0], got.shape[3]

    def body(got_ref, out_ref, wide_ref):
        wide_ref[...] = got_ref[...].astype(F32)
        for t in range(shards):
            for j in range(2):
                for c in range(2):
                    for i in range(2):
                        at = t * 8 + j * 4 + c * 2 + i
                        rows = wide_ref[pl.ds(at, pieces, stride=8 * shards), :]
                        cols = pl.ds((t * 2 + c) * width, width)
                        out_ref[j, pl.ds(i * pieces, pieces), cols] = rows.astype(BF16)

    vmem = pl.BlockSpec(memory_space=pltpu.VMEM)
    total = pieces * shards * 8
    return pl.pallas_call(
        body,
        out_shape=jax.ShapeDtypeStruct((2, 2 * pieces, shards * 2 * width), BF16),
        in_specs=[vmem],
        out_specs=vmem,
        scratch_shapes=[pltpu.VMEM((total, width), F32)],
        compiler_params=pltpu.CompilerParams(vmem_limit_bytes=16 * 1024 * 1024),
        name="placed",
    )(got.reshape(total, width))


def routed(directions, owner_table, row_blocks, col_blocks):
    slots = owner_table.shape[0]
    width = directions.shape[1]
    shards = lax.axis_size("tensor")
    held = lax.all_to_all(directions.reshape(slots, 8, width), DP, 0, 0, tiled=True)
    shape = (row_blocks, 4, 2, col_blocks, 2)
    r, q, j, c, i = (lax.broadcasted_iota(jnp.int32, shape, k) for k in range(5))
    wanted = ((((j * row_blocks + r) * col_blocks + c) * 4 + q) * 2 + i).reshape(-1)
    present = (owner_table[:, None] * 8 + jnp.arange(8, dtype=jnp.int32)[None, :]).reshape(-1)
    pick = (wanted[:, None] == present[None, :]).astype(BF16)
    chosen = jnp.dot(pick, held.reshape(slots * 8, width), preferred_element_type=F32)
    chosen = chosen.astype(BF16).reshape(slots, 1, 8, width)
    copies = jnp.broadcast_to(chosen, (slots, shards, 8, width)).reshape(slots * shards, 8, width)
    got = lax.all_to_all(copies, (*DP, "tensor"), 0, 0, tiled=True)
    return placed(got.reshape(slots, shards, 8, width), shards)


def own_gradient(activations, key_value_grads, owner_table, block_rows):
    tokens, features = activations.shape
    row_blocks = features // block_rows
    kvt = key_value_grads.reshape(tokens, -1).T
    acts_peer = swapped(activations)
    kvt_peer = swapped(kvt)

    four, two = ("fix", 4), ("fix", 2)
    first = [group_a(four, own(GIVE_Y + KEEP_Y)), group_b(two, own(GIVE_Z + KEEP_Z))]
    rest = [group_a(("sign", k), e) for k in (3, 2, 1) for e in (GIVE_Y, KEEP_Y)]
    rest += [group_b(("sign", 1), e) for e in (GIVE_Z, KEEP_Z)]
    rest += [group_a(("fix", 0), KEEP_Y), group_b(("fix", 0), KEEP_Z)]
    sizes = (block_rows, row_blocks, owner_table)
    sums = block_sums(first + rest, activations, kvt, *sizes)
    a4, b2 = block_sums(first, acts_peer, kvt_peer, *sizes, before=sums[:2])
    later = block_sums(rest, acts_peer, kvt_peer, *sizes, before=sums[2:])
    a3g, a3k, a2g, a2k, a1g, a1k, b1g, b1k, a0, b0 = later

    n_a, n_b = len(own(GIVE_Y)), len(own(GIVE_Z))
    b2 = directed(b2, Y)
    bg = added_inside(b1g, b2[:n_b], own_at(GIVE_Z))
    bk = added_inside(b1k, b2[n_b:], own_at(KEEP_Z))
    a4 = after(directed(a4, Z), bk)
    ag = added_inside(a3g, a4[:n_a], own_at(GIVE_Y))
    ak = added_inside(a3k, a4[n_a:], own_at(KEEP_Y))
    ag = added(a2g, after(directed(ag, Z), ak))
    bg = after(directed(bg, Y), ag)
    ak = added(a2k, after(directed(ak, Z), bg))
    ag = added(a1g, after(directed(ag, Z), ak))
    bk = after(directed(bk, Y), ag)
    b = wide(b0, bk, after(swapped(bg), bk))
    ak = added(a1k, after(directed(ak, Z), b))
    ag = after(directed(ag, Z), ak)
    b_far = after(directed(jnp.stack([b[3], b[0], b[5]]).astype(BF16), Z, 2), ag)
    b_two = jnp.stack([added(b[1], b_far[0]), b[6].astype(BF16)])
    b_one = jnp.stack([added(b[2], b_far[1]), added(b[7], b_far[2])])
    ak = after(directed(ak, Z), b_two)
    a = wide(a0, ak, after(swapped(ag), ak))
    a_two = a[1:2].astype(BF16)
    a_one = jnp.stack([a[0], a[3]]).astype(BF16)
    b_two = directed(b_two, Z, 2)
    b_one = directed(b_one, Z)
    a_two = directed(a_two, Y, 2)
    a_one = directed(a_one, Y)
    b_give = added(b_two[1], b_one[1])
    b_got = swapped(b_give)
    a_got = swapped(a_one[1])
    ga = [a[2], a_two[0], a_one[0], a_got]
    gb = [b[4], b_two[0], b_one[0], b_got]
    return ga, gb


def local(activations, key_value_grads, owner_table, left_factors, right_factors):
    rows_block = left_factors.shape[2]
    cols_block = right_factors.shape[2]
    row_blocks = activations.shape[1] // rows_block
    col_blocks = key_value_grads.shape[2] // cols_block
    inverse_tokens = 1.0 / (activations.shape[0] * lax.axis_size(DP))

    ga, gb = own_gradient(activations, key_value_grads, owner_table, rows_block)
    left_new, right_new, directions = precondition(
        ga, gb, left_factors[0, 0], right_factors[0, 0], inverse_tokens
    )
    update = routed(directions, owner_table, row_blocks, col_blocks)
    return (left_new[None, None], right_new[None, None], update)


def solution(mesh):
    split = Mesh(
        mesh.devices.reshape(8, 4, 2, mesh.shape["tensor"]), ("dp_0", "dp_1", "dp_2", "tensor")
    )
    return jax.shard_map(
        local,
        mesh=split,
        in_specs=(
            P(DP, None),
            P(DP, None, "tensor"),
            P(),
            P("tensor", DP, None, None),
            P("tensor", DP, None, None),
        ),
        out_specs=(P("tensor", DP, None, None), P("tensor", DP, None, None), P(None, DP, None)),
        check_vma=False,
    )
```

```python
import jax
import jax.numpy as jnp
from jax import lax
from jax.experimental import pallas as pl
from jax.experimental.pallas import tpu as pltpu
from jax.sharding import Mesh
from jax.sharding import PartitionSpec as P

ITERS = 8
NZ = 8
NY = 4
DP = ("dp_0", "dp_1", "dp_2")
Z, Y, CORE = DP
F32 = jnp.float32
BF16 = jnp.bfloat16
VMEM_LIMIT = 24 * 1024 * 1024

MOMENT_DECAY = 0.9
RIDGE_SHARE = 0.0001
def directed(x, axis, hops=1):
    size = lax.axis_size(axis)
    pairs = []
    for i in range(size):
        for core, step in enumerate((hops, -hops)):
            pairs.append((i * 2 + core, (i + step) % size * 2 + core))
    return lax.ppermute(x, (axis, CORE), pairs)


def shifted(x, axis, step):
    size = lax.axis_size(axis)
    return lax.ppermute(x, axis, [(i, (i + step) % size) for i in range(size)])


def swapped(x):
    return lax.ppermute(x, CORE, [(0, 1), (1, 0)])


def wide(*parts):
    total = parts[0].astype(F32)
    for p in parts[1:]:
        total = total + p.astype(F32)
    return total


def added(*parts):
    return wide(*parts).astype(BF16)


def added_inside(base, part, start):
    stop = start + part.shape[0]
    ends = [base[:start].astype(BF16), added(base[start:stop], part), base[stop:].astype(BF16)]
    return jnp.concatenate([e for e in ends if e.shape[0]], axis=0)


def after(x, *others):
    return lax.optimization_barrier((x, *others))[0]


def give_and_keep(near_offsets, fixed):
    back = [("sign", -k) for k in near_offsets]
    ahead = [("sign", k) for k in near_offsets]
    still = [("fix", k) for k in fixed]
    give = [(o, 1) for o in back + still] + [(o, 0) for o in back]
    keep = [(o, 0) for o in ahead + still] + [(o, 1) for o in ahead]
    return give, keep


GIVE_Y, KEEP_Y = give_and_keep((1,), (2, 0))
GIVE_Z, KEEP_Z = give_and_keep((3, 2, 1), (4, 0))


def own(entries):
    return [e for e in entries if e[1] == 0]


def own_at(entries):
    return entries.index(own(entries)[0])


def group_a(dz, entries):
    return [(0, dz, dy, flip) for dy, flip in entries]


def group_b(dy, entries):
    return [(1, dz, dy, flip) for dz, flip in entries]


def offset(what, size, core):
    kind, k = what
    if kind == "sign":
        return size + k - 2 * k * core
    return k


def block_sums(groups, acts, kvt, block_rows, row_blocks, owner_table, before=None):
    half_cols = block_rows // 2
    rows = kvt.shape[0] // 4
    held = F32 if before is None else BF16
    col_blocks = 2

    def body(owner_ref, a_ref, k_ref, *refs):
        base_refs = [] if before is None else refs[: len(groups)]
        out_refs = refs[len(base_refs) :]
        z, y, core = (lax.axis_index(a) for a in DP)
        for g, group in enumerate(groups):
            for n, (half, dz, dy, flip) in enumerate(group):
                to_z = dz[1] if dz[0] == "at" else (z + offset(dz, NZ, core)) % NZ
                to_y = (y + offset(dy, NY, core)) % NY
                to_core = core if flip == 0 else 1 - core
                block = owner_ref[(to_z * NY + to_y) * 2 + to_core]
                row = block // col_blocks % row_blocks
                line = block // (row_blocks * col_blocks) * col_blocks + block % col_blocks
                cols = pl.ds(pl.multiple_of((row * 2 + half) * half_cols, half_cols), half_cols)
                lines = pl.ds(pl.multiple_of(line * rows, rows), rows)
                summed = jnp.dot(k_ref[lines, :], a_ref[:, cols], preferred_element_type=F32)
                if before is not None:
                    summed = base_refs[g][n] + summed
                out_refs[g][n] = summed.astype(held)

    vmem = pl.BlockSpec(memory_space=pltpu.VMEM)
    smem = pl.BlockSpec(memory_space=pltpu.SMEM)
    inputs = [] if before is None else list(before)
    count = sum(len(g) for g in groups)
    moved = acts.size * 2 + kvt.size * 2 + count * rows * half_cols * (4 if before is None else 6)
    cost = pl.CostEstimate(
        flops=2 * count * rows * half_cols * acts.shape[0], transcendentals=0, bytes_accessed=moved
    )
    return pl.pallas_call(
        body,
        out_shape=[jax.ShapeDtypeStruct((len(g), rows, half_cols), held) for g in groups],
        in_specs=[smem, vmem, vmem] + [vmem] * len(inputs),
        out_specs=[vmem for _ in groups],
        compiler_params=pltpu.CompilerParams(vmem_limit_bytes=VMEM_LIMIT),
        cost_estimate=cost,
        name="block_sums",
    )(owner_table, acts, kvt, *inputs)


def transposed_sum(refs):
    total = refs[0][...].astype(F32)
    for ref in refs[1:]:
        total = total + ref[...].astype(F32)
    return total


def spread_eye(n):
    return lax.broadcasted_iota(jnp.int32, (n, n), 0) == lax.broadcasted_iota(jnp.int32, (n, n), 1)


def narrow_factor(powered, eye):
    return ((jnp.where(eye, 5.0, 0.0) - powered) * 0.25).astype(BF16)


def coarse(a, b):
    return jnp.dot(a, b, preferred_element_type=F32)


def exact(a, b):
    ah = a.astype(BF16)
    al = (a - ah.astype(F32)).astype(BF16)
    bh = b.astype(BF16)
    bl = (b - bh.astype(F32)).astype(BF16)
    return coarse(ah, bh) + (coarse(ah, bl) + coarse(al, bh))


def start_root(matrix, f_ref, m_ref, x_ref):
    n = matrix.shape[0]
    eye = spread_eye(n)
    trace = jnp.sum(jnp.where(eye, matrix, 0.0), keepdims=True)
    shifted = matrix + jnp.where(eye, RIDGE_SHARE * trace / n, 0.0)
    scaling = 2.5 / jnp.sqrt(jnp.sum(shifted * shifted, keepdims=True))
    powered = scaling * shifted
    factor = narrow_factor(powered, eye)
    first = jnp.sqrt(jnp.sqrt(scaling)).astype(BF16).astype(F32)
    f_ref[...] = factor
    m_ref[...] = powered.astype(BF16)
    x_ref[...] = jnp.where(eye, first, 0.0).astype(BF16)


def precondition(parts_a, parts_b, left, right, inverse_tokens):
    n_a, n_b = len(parts_a), len(parts_b)
    order, width = left.shape[0], right.shape[0]

    def body(*refs):
        a_refs, b_refs = refs[:n_a], refs[n_a : n_a + n_b]
        left_ref, right_ref, left_out, right_out, dir_ref = refs[n_a + n_b : n_a + n_b + 5]
        g_ref, spread_ref, fl, ml, xl, fr, mr, xr = refs[n_a + n_b + 5 :]
        gt = jnp.concatenate([transposed_sum(a_refs), transposed_sum(b_refs)], axis=1)
        gt = gt * inverse_tokens
        g = gt.T
        g_ref[...] = g
        share = 1.0 - MOMENT_DECAY
        left_new = MOMENT_DECAY * left_ref[...] + share * exact(g, gt)
        left_out[...] = left_new
        start_root(left_new, fl, ml, xl)
        right_new = MOMENT_DECAY * right_ref[...] + share * exact(gt, g)
        right_out[...] = right_new
        start_root(right_new, fr, mr, xr)

        eye_l, eye_r = spread_eye(order), spread_eye(width)
        for _ in range(ITERS - 1):
            factor_l, factor_r = fl[...], fr[...]
            squared_l = coarse(factor_l, factor_l).astype(BF16)
            squared_r = coarse(factor_r, factor_r).astype(BF16)
            xl[...] = coarse(xl[...], factor_l).astype(BF16)
            fourth_l = coarse(squared_l, squared_l).astype(BF16)
            fourth_r = coarse(squared_r, squared_r).astype(BF16)
            xr[...] = coarse(xr[...], factor_r).astype(BF16)
            powered_l = coarse(fourth_l, ml[...])
            powered_r = coarse(fourth_r, mr[...])
            fl[...] = narrow_factor(powered_l, eye_l)
            fr[...] = narrow_factor(powered_r, eye_r)
            ml[...] = powered_l.astype(BF16)
            mr[...] = powered_r.astype(BF16)
        left_root = coarse(xl[...], fl[...])
        right_root = coarse(xr[...], fr[...])
        pre = exact(exact(left_root, g_ref[...]), right_root)
        scale = jnp.sqrt(jnp.mean(pre * pre, keepdims=True) + 1e-06)
        g_ref[...] = pre / scale
        pieces = order // 8
        for q in range(4):
            for i in range(2):
                rows = g_ref[pl.ds((q * 2 + i) * pieces, pieces), :]
                spread_ref[pl.ds(q * 2 + i, pieces, stride=8), :] = rows
        dir_ref[...] = spread_ref[...].astype(BF16)

    vmem = pl.BlockSpec(memory_space=pltpu.VMEM)
    square = lambda n: [pltpu.VMEM((n, n), BF16)] * 3
    return pl.pallas_call(
        body,
        out_shape=[
            jax.ShapeDtypeStruct(left.shape, F32),
            jax.ShapeDtypeStruct(right.shape, F32),
            jax.ShapeDtypeStruct((order, width), BF16),
        ],
        in_specs=[vmem] * (n_a + n_b + 2),
        out_specs=[vmem] * 3,
        scratch_shapes=[pltpu.VMEM((order, width), F32)] * 2 + square(order) + square(width),
        compiler_params=pltpu.CompilerParams(vmem_limit_bytes=VMEM_LIMIT),
        name="precondition",
    )(*parts_a, *parts_b, left, right)

def placed(got, shards):
    pieces, width = got.shape[0], got.shape[3]

    def body(got_ref, out_ref, wide_ref):
        wide_ref[...] = got_ref[...].astype(F32)
        for t in range(shards):
            for j in range(2):
                for c in range(2):
                    for i in range(2):
                        at = t * 8 + j * 4 + c * 2 + i
                        rows = wide_ref[pl.ds(at, pieces, stride=8 * shards), :]
                        cols = pl.ds((t * 2 + c) * width, width)
                        out_ref[j, pl.ds(i * pieces, pieces), cols] = rows.astype(BF16)

    vmem = pl.BlockSpec(memory_space=pltpu.VMEM)
    total = pieces * shards * 8
    return pl.pallas_call(
        body,
        out_shape=jax.ShapeDtypeStruct((2, 2 * pieces, shards * 2 * width), BF16),
        in_specs=[vmem],
        out_specs=vmem,
        scratch_shapes=[pltpu.VMEM((total, width), F32)],
        compiler_params=pltpu.CompilerParams(vmem_limit_bytes=16 * 1024 * 1024),
        name="placed",
    )(got.reshape(total, width))


def routed(directions, owner_table, row_blocks, col_blocks):
    slots = owner_table.shape[0]
    width = directions.shape[1]
    shards = lax.axis_size("tensor")
    held = lax.all_to_all(directions.reshape(slots, 8, width), DP, 0, 0, tiled=True)
    shape = (row_blocks, 4, 2, col_blocks, 2)
    r, q, j, c, i = (lax.broadcasted_iota(jnp.int32, shape, k) for k in range(5))
    wanted = ((((j * row_blocks + r) * col_blocks + c) * 4 + q) * 2 + i).reshape(-1)
    present = (owner_table[:, None] * 8 + jnp.arange(8, dtype=jnp.int32)[None, :]).reshape(-1)
    pick = (wanted[:, None] == present[None, :]).astype(BF16)
    chosen = jnp.dot(pick, held.reshape(slots * 8, width), preferred_element_type=F32)
    chosen = chosen.astype(BF16).reshape(slots, 1, 8, width)
    copies = jnp.broadcast_to(chosen, (slots, shards, 8, width)).reshape(slots * shards, 8, width)
    got = lax.all_to_all(copies, (*DP, "tensor"), 0, 0, tiled=True)
    return placed(got.reshape(slots, shards, 8, width), shards)


def own_gradient(activations, key_value_grads, owner_table, block_rows):
    tokens, features = activations.shape
    row_blocks = features // block_rows
    kvt = key_value_grads.reshape(tokens, -1).T
    acts_peer = swapped(activations)
    kvt_peer = swapped(kvt)

    two = ("fix", 2)
    every = [(0, ("at", dz), ("fix", dy), 0) for dz in range(NZ) for dy in range(NY)]
    first = [every, group_b(two, own(GIVE_Z + KEEP_Z))]
    rest = [group_b(("sign", 1), GIVE_Z + KEEP_Z), group_b(("fix", 0), KEEP_Z)]
    sizes = (block_rows, row_blocks, owner_table)
    sums = block_sums(first + rest, activations, kvt, *sizes)
    a_all, b2 = block_sums(first, acts_peer, kvt_peer, *sizes, before=sums[:2])
    b1, b0 = block_sums(rest, acts_peer, kvt_peer, *sizes, before=sums[2:])

    a = lax.psum_scatter(a_all, Z, scatter_dimension=0, tiled=True)
    b_run = added_inside(b1, directed(b2, Y), own_at(GIVE_Z + KEEP_Z))
    b_run = directed(b_run, Y)
    n = len(GIVE_Z)
    b = wide(b0, b_run[n:], swapped(b_run[:n]))
    b_far = jnp.stack([b[3], b[0], b[5]]).astype(BF16)
    b_far = directed(b_far, Z, 2)
    b_two = jnp.stack([added(b[1], b_far[0]), b[6].astype(BF16)])
    b_one = jnp.stack([added(b[2], b_far[1]), added(b[7], b_far[2])])
    a = after(a, b_two)
    parts = [a[k] for k in range(4)]
    b_two = after(directed(b_two, Z, 2), *parts)
    b_one = after(directed(b_one, Z), *parts)
    ga = [parts[0]] + [shifted(parts[k], Y, k) for k in (2, 1, 3)]
    b_got = swapped(added(b_two[1], b_one[1]))
    gb = [b[4], b_two[0], b_one[0], b_got]
    return ga, gb


def local(activations, key_value_grads, owner_table, left_factors, right_factors):
    rows_block = left_factors.shape[2]
    cols_block = right_factors.shape[2]
    row_blocks = activations.shape[1] // rows_block
    col_blocks = key_value_grads.shape[2] // cols_block
    inverse_tokens = 1.0 / (activations.shape[0] * lax.axis_size(DP))

    ga, gb = own_gradient(activations, key_value_grads, owner_table, rows_block)
    left_new, right_new, directions = precondition(
        ga, gb, left_factors[0, 0], right_factors[0, 0], inverse_tokens
    )
    update = routed(directions, owner_table, row_blocks, col_blocks)
    return (left_new[None, None], right_new[None, None], update)


def solution(mesh):
    split = Mesh(
        mesh.devices.reshape(8, 4, 2, mesh.shape["tensor"]), ("dp_0", "dp_1", "dp_2", "tensor")
    )
    return jax.shard_map(
        local,
        mesh=split,
        in_specs=(
            P(DP, None),
            P(DP, None, "tensor"),
            P(),
            P("tensor", DP, None, None),
            P("tensor", DP, None, None),
        ),
        out_specs=(P("tensor", DP, None, None), P("tensor", DP, None, None), P(None, DP, None)),
        check_vma=False,
    )
```

```python
import jax
import jax.numpy as jnp
from jax import lax
from jax.experimental import pallas as pl
from jax.experimental.pallas import tpu as pltpu
from jax.sharding import Mesh
from jax.sharding import PartitionSpec as P

ITERS = 8
NZ = 8
NY = 4
DP = ("dp_0", "dp_1", "dp_2")
Z, Y, CORE = DP
F32 = jnp.float32
BF16 = jnp.bfloat16
VMEM_LIMIT = 24 * 1024 * 1024

MOMENT_DECAY = 0.9
RIDGE_SHARE = 0.0001
def directed(x, axis, hops=1):
    size = lax.axis_size(axis)
    pairs = []
    for i in range(size):
        for core, step in enumerate((hops, -hops)):
            pairs.append((i * 2 + core, (i + step) % size * 2 + core))
    return lax.ppermute(x, (axis, CORE), pairs)


def swapped(x):
    return lax.ppermute(x, CORE, [(0, 1), (1, 0)])


def wide(*parts):
    total = parts[0].astype(F32)
    for p in parts[1:]:
        total = total + p.astype(F32)
    return total


def added(*parts):
    return wide(*parts).astype(BF16)


def added_inside(base, part, start):
    stop = start + part.shape[0]
    ends = [base[:start].astype(BF16), added(base[start:stop], part), base[stop:].astype(BF16)]
    return jnp.concatenate([e for e in ends if e.shape[0]], axis=0)


def after(x, *others):
    return lax.optimization_barrier((x, *others))[0]


def give_and_keep(near_offsets, fixed):
    back = [("sign", -k) for k in near_offsets]
    ahead = [("sign", k) for k in near_offsets]
    still = [("fix", k) for k in fixed]
    give = [(o, 1) for o in back + still] + [(o, 0) for o in back]
    keep = [(o, 0) for o in ahead + still] + [(o, 1) for o in ahead]
    return give, keep


GIVE_Y, KEEP_Y = give_and_keep((1,), (2, 0))
GIVE_Z, KEEP_Z = give_and_keep((3, 2, 1), (4, 0))


def own(entries):
    return [e for e in entries if e[1] == 0]


def own_at(entries):
    return entries.index(own(entries)[0])


def group_a(dz, entries):
    return [(0, dz, dy, flip) for dy, flip in entries]


def group_b(dy, entries):
    return [(1, dz, dy, flip) for dz, flip in entries]


def offset(what, size, core):
    kind, k = what
    if kind == "sign":
        return size + k - 2 * k * core
    return k


def block_sums(groups, acts, kvt, block_rows, row_blocks, owner_table, before=None, fetch=False):
    half_cols = block_rows // 2
    rows = kvt.shape[0] // 4
    held = F32 if before is None else BF16
    col_blocks = 2

    def body(owner_ref, a_ref, k_ref, *refs):
        base_refs = [] if before is None else refs[: len(groups)]
        out_refs = refs[len(base_refs) : len(base_refs) + len(groups)]
        z, y, core = (lax.axis_index(a) for a in DP)
        work = []
        for g, group in enumerate(groups):
            for n, (half, dz, dy, flip) in enumerate(group):
                to_z = (z + offset(dz, NZ, core)) % NZ
                to_y = (y + offset(dy, NY, core)) % NY
                to_core = core if flip == 0 else 1 - core
                block = owner_ref[(to_z * NY + to_y) * 2 + to_core]
                row = block // col_blocks % row_blocks
                line = block // (row_blocks * col_blocks) * col_blocks + block % col_blocks
                cols = pl.ds(pl.multiple_of((row * 2 + half) * half_cols, half_cols), half_cols)
                lines = pl.ds(pl.multiple_of(line * rows, rows), rows)
                work.append((g, n, cols, lines))
        if fetch:
            held_ref, sems = refs[-2:]
            copies = [
                pltpu.make_async_copy(a_ref.at[:, w[2]], held_ref.at[k], sems.at[k])
                for k, w in enumerate(work)
            ]
            for copy in copies:
                copy.start()
        for k, (g, n, cols, lines) in enumerate(work):
            if fetch:
                copies[k].wait()
                part = held_ref[k]
            else:
                part = a_ref[:, cols]
            summed = jnp.dot(k_ref[lines, :], part, preferred_element_type=F32)
            if before is not None:
                summed = base_refs[g][n] + summed
            out_refs[g][n] = summed.astype(held)

    vmem = pl.BlockSpec(memory_space=pltpu.VMEM)
    smem = pl.BlockSpec(memory_space=pltpu.SMEM)
    inputs = [] if before is None else list(before)
    count = sum(len(g) for g in groups)
    scratch = []
    if fetch:
        scratch = [pltpu.VMEM((count, acts.shape[0], half_cols), BF16)]
        scratch.append(pltpu.SemaphoreType.DMA((count,)))
    moved = acts.size * 2 + kvt.size * 2 + count * rows * half_cols * (4 if before is None else 6)
    cost = pl.CostEstimate(
        flops=2 * count * rows * half_cols * acts.shape[0], transcendentals=0, bytes_accessed=moved
    )
    return pl.pallas_call(
        body,
        out_shape=[jax.ShapeDtypeStruct((len(g), rows, half_cols), held) for g in groups],
        in_specs=[smem, pl.BlockSpec(memory_space=pl.ANY) if fetch else vmem, vmem] + [vmem] * len(inputs),
        out_specs=[vmem for _ in groups],
        scratch_shapes=scratch,
        compiler_params=pltpu.CompilerParams(vmem_limit_bytes=VMEM_LIMIT),
        cost_estimate=cost,
        name="block_sums",
    )(owner_table, acts, kvt, *inputs)


def transposed_sum(refs):
    total = refs[0][...].astype(F32)
    for ref in refs[1:]:
        total = total + ref[...].astype(F32)
    return total


def spread_eye(n):
    return lax.broadcasted_iota(jnp.int32, (n, n), 0) == lax.broadcasted_iota(jnp.int32, (n, n), 1)


def narrow_factor(powered, eye):
    return ((jnp.where(eye, 5.0, 0.0) - powered) * 0.25).astype(BF16)


def coarse(a, b):
    return jnp.dot(a, b, preferred_element_type=F32)


def exact(a, b):
    ah = a.astype(BF16)
    al = (a - ah.astype(F32)).astype(BF16)
    bh = b.astype(BF16)
    bl = (b - bh.astype(F32)).astype(BF16)
    return coarse(ah, bh) + (coarse(ah, bl) + coarse(al, bh))


def start_root(matrix, f_ref, m_ref, x_ref):
    n = matrix.shape[0]
    eye = spread_eye(n)
    trace = jnp.sum(jnp.where(eye, matrix, 0.0), keepdims=True)
    shifted = matrix + jnp.where(eye, RIDGE_SHARE * trace / n, 0.0)
    scaling = 2.5 / jnp.sqrt(jnp.sum(shifted * shifted, keepdims=True))
    powered = scaling * shifted
    factor = narrow_factor(powered, eye)
    first = jnp.sqrt(jnp.sqrt(scaling)).astype(BF16).astype(F32)
    f_ref[...] = factor
    m_ref[...] = powered.astype(BF16)
    x_ref[...] = jnp.where(eye, first, 0.0).astype(BF16)


def precondition(parts_a, parts_b, left, right, inverse_tokens):
    n_a, n_b = len(parts_a), len(parts_b)
    order, width = left.shape[0], right.shape[0]

    def body(*refs):
        a_refs, b_refs = refs[:n_a], refs[n_a : n_a + n_b]
        left_ref, right_ref, left_out, right_out, dir_ref = refs[n_a + n_b : n_a + n_b + 5]
        g_ref, spread_ref, fl, ml, xl, fr, mr, xr = refs[n_a + n_b + 5 :]
        gt = jnp.concatenate([transposed_sum(a_refs), transposed_sum(b_refs)], axis=1)
        gt = gt * inverse_tokens
        g = gt.T
        g_ref[...] = g
        share = 1.0 - MOMENT_DECAY
        left_new = MOMENT_DECAY * left_ref[...] + share * exact(g, gt)
        left_out[...] = left_new
        start_root(left_new, fl, ml, xl)
        right_new = MOMENT_DECAY * right_ref[...] + share * exact(gt, g)
        right_out[...] = right_new
        start_root(right_new, fr, mr, xr)

        eye_l, eye_r = spread_eye(order), spread_eye(width)
        for _ in range(ITERS - 1):
            factor_l, factor_r = fl[...], fr[...]
            squared_l = coarse(factor_l, factor_l).astype(BF16)
            squared_r = coarse(factor_r, factor_r).astype(BF16)
            xl[...] = coarse(xl[...], factor_l).astype(BF16)
            fourth_l = coarse(squared_l, squared_l).astype(BF16)
            fourth_r = coarse(squared_r, squared_r).astype(BF16)
            xr[...] = coarse(xr[...], factor_r).astype(BF16)
            powered_l = coarse(fourth_l, ml[...])
            powered_r = coarse(fourth_r, mr[...])
            fl[...] = narrow_factor(powered_l, eye_l)
            fr[...] = narrow_factor(powered_r, eye_r)
            ml[...] = powered_l.astype(BF16)
            mr[...] = powered_r.astype(BF16)
        left_root = coarse(xl[...], fl[...])
        right_root = coarse(xr[...], fr[...])
        pre = exact(exact(left_root, g_ref[...]), right_root)
        scale = jnp.sqrt(jnp.mean(pre * pre, keepdims=True) + 1e-06)
        g_ref[...] = pre / scale
        pieces = order // 8
        for q in range(4):
            for i in range(2):
                rows = g_ref[pl.ds((q * 2 + i) * pieces, pieces), :]
                spread_ref[pl.ds(q * 2 + i, pieces, stride=8), :] = rows
        dir_ref[...] = spread_ref[...].astype(BF16)

    vmem = pl.BlockSpec(memory_space=pltpu.VMEM)
    square = lambda n: [pltpu.VMEM((n, n), BF16)] * 3
    return pl.pallas_call(
        body,
        out_shape=[
            jax.ShapeDtypeStruct(left.shape, F32),
            jax.ShapeDtypeStruct(right.shape, F32),
            jax.ShapeDtypeStruct((order, width), BF16),
        ],
        in_specs=[vmem] * (n_a + n_b + 2),
        out_specs=[vmem] * 3,
        scratch_shapes=[pltpu.VMEM((order, width), F32)] * 2 + square(order) + square(width),
        compiler_params=pltpu.CompilerParams(vmem_limit_bytes=VMEM_LIMIT),
        name="precondition",
    )(*parts_a, *parts_b, left, right)

def placed(got, shards):
    pieces, width = got.shape[0], got.shape[3]

    def body(got_ref, out_ref, wide_ref):
        wide_ref[...] = got_ref[...].astype(F32)
        for t in range(shards):
            for j in range(2):
                for c in range(2):
                    for i in range(2):
                        at = t * 8 + j * 4 + c * 2 + i
                        rows = wide_ref[pl.ds(at, pieces, stride=8 * shards), :]
                        cols = pl.ds((t * 2 + c) * width, width)
                        out_ref[j, pl.ds(i * pieces, pieces), cols] = rows.astype(BF16)

    vmem = pl.BlockSpec(memory_space=pltpu.VMEM)
    total = pieces * shards * 8
    return pl.pallas_call(
        body,
        out_shape=jax.ShapeDtypeStruct((2, 2 * pieces, shards * 2 * width), BF16),
        in_specs=[vmem],
        out_specs=vmem,
        scratch_shapes=[pltpu.VMEM((total, width), F32)],
        compiler_params=pltpu.CompilerParams(vmem_limit_bytes=16 * 1024 * 1024),
        name="placed",
    )(got.reshape(total, width))


def routed(directions, owner_table, row_blocks, col_blocks):
    slots = owner_table.shape[0]
    width = directions.shape[1]
    shards = lax.axis_size("tensor")
    held = lax.all_to_all(directions.reshape(slots, 8, width), DP, 0, 0, tiled=True)
    shape = (row_blocks, 4, 2, col_blocks, 2)
    r, q, j, c, i = (lax.broadcasted_iota(jnp.int32, shape, k) for k in range(5))
    wanted = ((((j * row_blocks + r) * col_blocks + c) * 4 + q) * 2 + i).reshape(-1)
    present = (owner_table[:, None] * 8 + jnp.arange(8, dtype=jnp.int32)[None, :]).reshape(-1)
    pick = (wanted[:, None] == present[None, :]).astype(BF16)
    chosen = jnp.dot(pick, held.reshape(slots * 8, width), preferred_element_type=F32)
    chosen = chosen.astype(BF16).reshape(slots, 1, 8, width)
    copies = jnp.broadcast_to(chosen, (slots, shards, 8, width)).reshape(slots * shards, 8, width)
    got = lax.all_to_all(copies, (*DP, "tensor"), 0, 0, tiled=True)
    return placed(got.reshape(slots, shards, 8, width), shards)


def own_gradient(activations, key_value_grads, owner_table, block_rows):
    tokens, features = activations.shape
    row_blocks = features // block_rows
    kvt = key_value_grads.reshape(tokens, -1).T
    acts_peer = swapped(activations)
    kvt_peer = swapped(kvt)

    four, two = ("fix", 4), ("fix", 2)
    first = [group_a(four, own(GIVE_Y + KEEP_Y)), group_b(two, own(GIVE_Z + KEEP_Z))]
    first += [group_a(("sign", 3), e) for e in (GIVE_Y, KEEP_Y)]
    rest = [group_a(("sign", k), e) for k in (2, 1) for e in (GIVE_Y, KEEP_Y)]
    rest += [group_b(("sign", 1), e) for e in (GIVE_Z, KEEP_Z)]
    rest += [group_a(("fix", 0), KEEP_Y), group_b(("fix", 0), KEEP_Z)]
    sizes = (block_rows, row_blocks, owner_table)
    sums = block_sums(first + rest, activations, kvt, *sizes)
    a4, b2, a3g, a3k = block_sums(
        first, acts_peer, kvt_peer, *sizes, before=sums[:4], fetch=True
    )
    later = block_sums(rest, acts_peer, kvt_peer, *sizes, before=sums[4:])
    a2g, a2k, a1g, a1k, b1g, b1k, a0, b0 = later

    n_a, n_b = len(own(GIVE_Y)), len(own(GIVE_Z))
    a4 = directed(a4, Z, 2)
    b2 = after(directed(b2, Y), a4)
    bg = added_inside(b1g, b2[:n_b], own_at(GIVE_Z))
    bk = added_inside(b1k, after(b2[n_b:], bg), own_at(KEEP_Z))
    ag = added_inside(wide(a2g, after(directed(a3g, Z), bk)), a4[:n_a], own_at(GIVE_Y))
    ak = added_inside(wide(a2k, after(directed(a3k, Z), ag)), a4[n_a:], own_at(KEEP_Y))
    bg = after(directed(bg, Y), ak)
    ag = added(a1g, after(directed(ag, Z), bg))
    bk = after(directed(bk, Y), ag)
    b = wide(b0, bk, after(swapped(bg), bk))
    ak = added(a1k, after(directed(ak, Z), b))
    ag = after(directed(ag, Z), ak)
    b_far = after(directed(jnp.stack([b[3], b[0], b[5]]).astype(BF16), Z, 2), ag)
    b_two = jnp.stack([added(b[1], b_far[0]), b[6].astype(BF16)])
    b_one = jnp.stack([added(b[2], b_far[1]), added(b[7], b_far[2])])
    ak = after(directed(ak, Z), b_two)
    a = wide(a0, ak, after(swapped(ag), ak))
    a_two = a[1:2].astype(BF16)
    a_one = jnp.stack([a[0], a[3]]).astype(BF16)
    b_two = directed(b_two, Z, 2)
    b_one = directed(b_one, Z)
    a_two = directed(a_two, Y, 2)
    a_one = directed(a_one, Y)
    b_give = added(b_two[1], b_one[1])
    b_got = swapped(b_give)
    a_got = swapped(a_one[1])
    ga = [a[2], a_two[0], a_one[0], a_got]
    gb = [b[4], b_two[0], b_one[0], b_got]
    return ga, gb


def local(activations, key_value_grads, owner_table, left_factors, right_factors):
    rows_block = left_factors.shape[2]
    cols_block = right_factors.shape[2]
    row_blocks = activations.shape[1] // rows_block
    col_blocks = key_value_grads.shape[2] // cols_block
    inverse_tokens = 1.0 / (activations.shape[0] * lax.axis_size(DP))

    ga, gb = own_gradient(activations, key_value_grads, owner_table, rows_block)
    left_new, right_new, directions = precondition(
        ga, gb, left_factors[0, 0], right_factors[0, 0], inverse_tokens
    )
    update = routed(directions, owner_table, row_blocks, col_blocks)
    return (left_new[None, None], right_new[None, None], update)


def solution(mesh):
    split = Mesh(
        mesh.devices.reshape(8, 4, 2, mesh.shape["tensor"]), ("dp_0", "dp_1", "dp_2", "tensor")
    )
    return jax.shard_map(
        local,
        mesh=split,
        in_specs=(
            P(DP, None),
            P(DP, None, "tensor"),
            P(),
            P("tensor", DP, None, None),
            P("tensor", DP, None, None),
        ),
        out_specs=(P("tensor", DP, None, None), P("tensor", DP, None, None), P(None, DP, None)),
        check_vma=False,
    )
```

```python
import jax
import jax.numpy as jnp
from jax import lax
from jax.experimental import pallas as pl
from jax.experimental.pallas import tpu as pltpu
from jax.sharding import Mesh
from jax.sharding import PartitionSpec as P

ITERS = 8
NZ = 8
NY = 4
DP = ("dp_0", "dp_1", "dp_2")
Z, Y, CORE = DP
F32 = jnp.float32
BF16 = jnp.bfloat16
VMEM_LIMIT = 24 * 1024 * 1024

MOMENT_DECAY = 0.9
RIDGE_SHARE = 0.0001
def directed(x, axis, hops=1):
    size = lax.axis_size(axis)
    pairs = []
    for i in range(size):
        for core, step in enumerate((hops, -hops)):
            pairs.append((i * 2 + core, (i + step) % size * 2 + core))
    return lax.ppermute(x, (axis, CORE), pairs)


def swapped(x):
    return lax.ppermute(x, CORE, [(0, 1), (1, 0)])


def wide(*parts):
    total = parts[0].astype(F32)
    for p in parts[1:]:
        total = total + p.astype(F32)
    return total


def added(*parts):
    return wide(*parts).astype(BF16)


def added_inside(base, part, start):
    stop = start + part.shape[0]
    ends = [base[:start].astype(BF16), added(base[start:stop], part), base[stop:].astype(BF16)]
    return jnp.concatenate([e for e in ends if e.shape[0]], axis=0)


def after(x, *others):
    return lax.optimization_barrier((x, *others))[0]


def give_and_keep(near_offsets, fixed):
    back = [("sign", -k) for k in near_offsets]
    ahead = [("sign", k) for k in near_offsets]
    still = [("fix", k) for k in fixed]
    give = [(o, 1) for o in back + still] + [(o, 0) for o in back]
    keep = [(o, 0) for o in ahead + still] + [(o, 1) for o in ahead]
    return give, keep


GIVE_Y, KEEP_Y = give_and_keep((1,), (2, 0))
GIVE_Z, KEEP_Z = give_and_keep((3, 2, 1), (4, 0))


def own(entries):
    return [e for e in entries if e[1] == 0]


def own_at(entries):
    return entries.index(own(entries)[0])


def group_a(dz, entries):
    return [(0, dz, dy, flip) for dy, flip in entries]


def group_b(dy, entries):
    return [(1, dz, dy, flip) for dz, flip in entries]


def offset(what, size, core):
    kind, k = what
    if kind == "sign":
        return size + k - 2 * k * core
    return k


def block_sums(groups, acts, kvt, block_rows, row_blocks, owner_table, before=None):
    half_cols = block_rows // 2
    rows = kvt.shape[0] // 4
    held = F32 if before is None else BF16
    col_blocks = 2

    def body(owner_ref, a_ref, k_ref, *refs):
        base_refs = [] if before is None else refs[: len(groups)]
        out_refs = refs[len(base_refs) : len(base_refs) + len(groups)]
        z, y, core = (lax.axis_index(a) for a in DP)
        work = []
        for g, group in enumerate(groups):
            for n, (half, dz, dy, flip) in enumerate(group):
                to_z = (z + offset(dz, NZ, core)) % NZ
                to_y = (y + offset(dy, NY, core)) % NY
                to_core = core if flip == 0 else 1 - core
                block = owner_ref[(to_z * NY + to_y) * 2 + to_core]
                row = block // col_blocks % row_blocks
                line = block // (row_blocks * col_blocks) * col_blocks + block % col_blocks
                cols = pl.ds(pl.multiple_of((row * 2 + half) * half_cols, half_cols), half_cols)
                lines = pl.ds(pl.multiple_of(line * rows, rows), rows)
                work.append((g, n, cols, lines))
        for g, n, cols, lines in work:
            summed = jnp.dot(k_ref[lines, :], a_ref[:, cols], preferred_element_type=F32)
            if before is not None:
                summed = base_refs[g][n] + summed
            out_refs[g][n] = summed.astype(held)

    vmem = pl.BlockSpec(memory_space=pltpu.VMEM)
    smem = pl.BlockSpec(memory_space=pltpu.SMEM)
    inputs = [] if before is None else list(before)
    count = sum(len(g) for g in groups)
    moved = acts.size * 2 + kvt.size * 2 + count * rows * half_cols * (4 if before is None else 6)
    cost = pl.CostEstimate(
        flops=2 * count * rows * half_cols * acts.shape[0], transcendentals=0, bytes_accessed=moved
    )
    return pl.pallas_call(
        body,
        out_shape=[jax.ShapeDtypeStruct((len(g), rows, half_cols), held) for g in groups],
        in_specs=[smem, vmem, vmem] + [vmem] * len(inputs),
        out_specs=[vmem for _ in groups],
        compiler_params=pltpu.CompilerParams(vmem_limit_bytes=VMEM_LIMIT),
        cost_estimate=cost,
        name="block_sums",
    )(owner_table, acts, kvt, *inputs)


def transposed_sum(refs):
    total = refs[0][...].astype(F32)
    for ref in refs[1:]:
        total = total + ref[...].astype(F32)
    return total


def spread_eye(n):
    return lax.broadcasted_iota(jnp.int32, (n, n), 0) == lax.broadcasted_iota(jnp.int32, (n, n), 1)


def narrow_factor(powered, eye):
    return ((jnp.where(eye, 5.0, 0.0) - powered) * 0.25).astype(BF16)


def coarse(a, b):
    return jnp.dot(a, b, preferred_element_type=F32)


def exact(a, b):
    ah = a.astype(BF16)
    al = (a - ah.astype(F32)).astype(BF16)
    bh = b.astype(BF16)
    bl = (b - bh.astype(F32)).astype(BF16)
    return coarse(ah, bh) + (coarse(ah, bl) + coarse(al, bh))


def start_root(matrix, f_ref, m_ref, x_ref):
    n = matrix.shape[0]
    eye = spread_eye(n)
    trace = jnp.sum(jnp.where(eye, matrix, 0.0), keepdims=True)
    shifted = matrix + jnp.where(eye, RIDGE_SHARE * trace / n, 0.0)
    scaling = 2.5 / jnp.sqrt(jnp.sum(shifted * shifted, keepdims=True))
    powered = scaling * shifted
    factor = narrow_factor(powered, eye)
    first = jnp.sqrt(jnp.sqrt(scaling)).astype(BF16).astype(F32)
    f_ref[...] = factor
    m_ref[...] = powered.astype(BF16)
    x_ref[...] = jnp.where(eye, first, 0.0).astype(BF16)


def precondition(parts_a, parts_b, left, right, inverse_tokens):
    n_a, n_b = len(parts_a), len(parts_b)
    order, width = left.shape[0], right.shape[0]

    def body(*refs):
        a_refs, b_refs = refs[:n_a], refs[n_a : n_a + n_b]
        left_ref, right_ref, left_out, right_out, dir_ref = refs[n_a + n_b : n_a + n_b + 5]
        g_ref, spread_ref, fl, ml, xl, fr, mr, xr = refs[n_a + n_b + 5 :]
        gt = jnp.concatenate([transposed_sum(a_refs), transposed_sum(b_refs)], axis=1)
        gt = gt * inverse_tokens
        g = gt.T
        g_ref[...] = g
        share = 1.0 - MOMENT_DECAY
        left_new = MOMENT_DECAY * left_ref[...] + share * exact(g, gt)
        left_out[...] = left_new
        start_root(left_new, fl, ml, xl)
        right_new = MOMENT_DECAY * right_ref[...] + share * exact(gt, g)
        right_out[...] = right_new
        start_root(right_new, fr, mr, xr)

        eye_l, eye_r = spread_eye(order), spread_eye(width)
        for _ in range(ITERS - 1):
            factor_l, factor_r = fl[...], fr[...]
            squared_l = coarse(factor_l, factor_l).astype(BF16)
            squared_r = coarse(factor_r, factor_r).astype(BF16)
            xl[...] = coarse(xl[...], factor_l).astype(BF16)
            fourth_l = coarse(squared_l, squared_l).astype(BF16)
            fourth_r = coarse(squared_r, squared_r).astype(BF16)
            xr[...] = coarse(xr[...], factor_r).astype(BF16)
            powered_l = coarse(fourth_l, ml[...])
            powered_r = coarse(fourth_r, mr[...])
            fl[...] = narrow_factor(powered_l, eye_l)
            fr[...] = narrow_factor(powered_r, eye_r)
            ml[...] = powered_l.astype(BF16)
            mr[...] = powered_r.astype(BF16)
        left_root = coarse(xl[...], fl[...])
        right_root = coarse(xr[...], fr[...])
        pre = exact(exact(left_root, g_ref[...]), right_root)
        scale = jnp.sqrt(jnp.mean(pre * pre, keepdims=True) + 1e-06)
        g_ref[...] = pre / scale
        pieces = order // 8
        for q in range(4):
            for i in range(2):
                rows = g_ref[pl.ds((q * 2 + i) * pieces, pieces), :]
                spread_ref[pl.ds(q * 2 + i, pieces, stride=8), :] = rows
        dir_ref[...] = spread_ref[...].astype(BF16)

    vmem = pl.BlockSpec(memory_space=pltpu.VMEM)
    square = lambda n: [pltpu.VMEM((n, n), BF16)] * 3
    return pl.pallas_call(
        body,
        out_shape=[
            jax.ShapeDtypeStruct(left.shape, F32),
            jax.ShapeDtypeStruct(right.shape, F32),
            jax.ShapeDtypeStruct((order, width), BF16),
        ],
        in_specs=[vmem] * (n_a + n_b + 2),
        out_specs=[vmem] * 3,
        scratch_shapes=[pltpu.VMEM((order, width), F32)] * 2 + square(order) + square(width),
        compiler_params=pltpu.CompilerParams(vmem_limit_bytes=VMEM_LIMIT),
        name="precondition",
    )(*parts_a, *parts_b, left, right)

def placed(got, shards):
    pieces, width = got.shape[0], got.shape[3]

    def body(got_ref, out_ref, wide_ref):
        wide_ref[...] = got_ref[...].astype(F32)
        for t in range(shards):
            for j in range(2):
                for c in range(2):
                    for i in range(2):
                        at = t * 8 + j * 4 + c * 2 + i
                        rows = wide_ref[pl.ds(at, pieces, stride=8 * shards), :]
                        cols = pl.ds((t * 2 + c) * width, width)
                        out_ref[j, pl.ds(i * pieces, pieces), cols] = rows.astype(BF16)

    vmem = pl.BlockSpec(memory_space=pltpu.VMEM)
    total = pieces * shards * 8
    return pl.pallas_call(
        body,
        out_shape=jax.ShapeDtypeStruct((2, 2 * pieces, shards * 2 * width), BF16),
        in_specs=[vmem],
        out_specs=vmem,
        scratch_shapes=[pltpu.VMEM((total, width), F32)],
        compiler_params=pltpu.CompilerParams(vmem_limit_bytes=16 * 1024 * 1024),
        name="placed",
    )(got.reshape(total, width))


def routed(directions, owner_table, row_blocks, col_blocks):
    slots = owner_table.shape[0]
    width = directions.shape[1]
    shards = lax.axis_size("tensor")
    held = lax.all_to_all(directions.reshape(slots, 8, width), DP, 0, 0, tiled=True)
    shape = (row_blocks, 4, 2, col_blocks, 2)
    r, q, j, c, i = (lax.broadcasted_iota(jnp.int32, shape, k) for k in range(5))
    wanted = ((((j * row_blocks + r) * col_blocks + c) * 4 + q) * 2 + i).reshape(-1)
    present = (owner_table[:, None] * 8 + jnp.arange(8, dtype=jnp.int32)[None, :]).reshape(-1)
    pick = (wanted[:, None] == present[None, :]).astype(BF16)
    chosen = jnp.dot(pick, held.reshape(slots * 8, width), preferred_element_type=F32)
    chosen = chosen.astype(BF16).reshape(slots, 1, 8, width)
    copies = jnp.broadcast_to(chosen, (slots, shards, 8, width)).reshape(slots * shards, 8, width)
    got = lax.all_to_all(copies, (*DP, "tensor"), 0, 0, tiled=True)
    return placed(got.reshape(slots, shards, 8, width), shards)


def own_gradient(activations, key_value_grads, owner_table, block_rows):
    tokens, features = activations.shape
    row_blocks = features // block_rows
    kvt = key_value_grads.reshape(tokens, -1).T
    acts_peer = swapped(activations)
    kvt_peer = swapped(kvt)

    four, two = ("fix", 4), ("fix", 2)
    first = [group_a(four, own(GIVE_Y + KEEP_Y)), group_b(two, own(GIVE_Z + KEEP_Z))]
    first += [group_a(("sign", 3), e) for e in (GIVE_Y, KEEP_Y)]
    rest = [group_a(("sign", k), e) for k in (2, 1) for e in (GIVE_Y, KEEP_Y)]
    rest += [group_b(("sign", 1), e) for e in (GIVE_Z, KEEP_Z)]
    rest += [group_a(("fix", 0), KEEP_Y), group_b(("fix", 0), KEEP_Z)]
    sizes = (block_rows, row_blocks, owner_table)
    sums = block_sums(first + rest, activations, kvt, *sizes)
    a4, b2, a3g, a3k = block_sums(first, acts_peer, kvt_peer, *sizes, before=sums[:4])
    later = block_sums(rest, acts_peer, kvt_peer, *sizes, before=sums[4:])
    a2g, a2k, a1g, a1k, b1g, b1k, a0, b0 = later

    n_a, n_b = len(own(GIVE_Y)), len(own(GIVE_Z))
    a4 = directed(a4, Z, 2)
    b2 = after(directed(b2, Y), a4)
    bg = added_inside(b1g, b2[:n_b], own_at(GIVE_Z))
    bk = added_inside(b1k, after(b2[n_b:], bg), own_at(KEEP_Z))
    ag = added_inside(wide(a2g, after(directed(a3g, Z), bk)), a4[:n_a], own_at(GIVE_Y))
    ak = added_inside(wide(a2k, after(directed(a3k, Z), ag)), a4[n_a:], own_at(KEEP_Y))
    bg = after(directed(bg, Y), ak)
    ag = added(a1g, after(directed(ag, Z), bg))
    bk = after(directed(bk, Y), ag)
    b = wide(b0, bk, after(swapped(bg), bk))
    ak = added(a1k, after(directed(ak, Z), b))
    ag = after(directed(ag, Z), ak)
    b_far = after(directed(jnp.stack([b[3], b[0], b[5]]).astype(BF16), Z, 2), ag)
    b_two = jnp.stack([added(b[1], b_far[0]), b[6].astype(BF16)])
    b_one = jnp.stack([added(b[2], b_far[1]), added(b[7], b_far[2])])
    ak = after(directed(ak, Z), b_two)
    a = wide(a0, ak, after(swapped(ag), ak))
    a_two = a[1:2].astype(BF16)
    a_one = jnp.stack([a[0], a[3]]).astype(BF16)
    b_two = directed(b_two, Z, 2)
    b_one = directed(b_one, Z)
    a_two = directed(a_two, Y, 2)
    a_one = directed(a_one, Y)
    b_give = added(b_two[1], b_one[1])
    b_got = swapped(b_give)
    a_got = swapped(a_one[1])
    ga = [a[2], a_two[0], a_one[0], a_got]
    gb = [b[4], b_two[0], b_one[0], b_got]
    return ga, gb


def local(activations, key_value_grads, owner_table, left_factors, right_factors):
    rows_block = left_factors.shape[2]
    cols_block = right_factors.shape[2]
    row_blocks = activations.shape[1] // rows_block
    col_blocks = key_value_grads.shape[2] // cols_block
    inverse_tokens = 1.0 / (activations.shape[0] * lax.axis_size(DP))

    ga, gb = own_gradient(activations, key_value_grads, owner_table, rows_block)
    left_new, right_new, directions = precondition(
        ga, gb, left_factors[0, 0], right_factors[0, 0], inverse_tokens
    )
    update = routed(directions, owner_table, row_blocks, col_blocks)
    return (left_new[None, None], right_new[None, None], update)


def solution(mesh):
    split = Mesh(
        mesh.devices.reshape(8, 4, 2, mesh.shape["tensor"]), ("dp_0", "dp_1", "dp_2", "tensor")
    )
    return jax.shard_map(
        local,
        mesh=split,
        in_specs=(
            P(DP, None),
            P(DP, None, "tensor"),
            P(),
            P("tensor", DP, None, None),
            P("tensor", DP, None, None),
        ),
        out_specs=(P("tensor", DP, None, None), P("tensor", DP, None, None), P(None, DP, None)),
        check_vma=False,
    )
```
